32 devices in a mesh: dp: 8 (over z, x), tile: 4 (over y, core).
Axes of the slice: x: 2, y: 2, z: 4, core: 2. Of those that a mesh axis runs over, the one named last changes fastest.
Arguments:
- frames: bfloat16 [32, 4, 64, 256], P('dp', 'tile'), may hold values from -6 to 6
- kernels: bfloat16 [32, 9, 256, 256], P('dp'), may hold values from -0.125 to 0.125
- experts: int32 [32, 4, 4], P('dp', 'tile'), may hold values from 0 to 31, as said below
- counts: int32 [32, 4], P('dp', 'tile'), may hold values from 2 to 4
- gate_weights: float32 [32, 4, 4], P('dp', 'tile'), may hold values from 0.25 to 1
- cotangent: bfloat16 [32, 4, 64, 256], P('dp', 'tile'), may hold values from -6 to 6
Outputs:
- frames_out: bfloat16 [32, 4, 64, 256], P('dp', 'tile')
- input_grad: bfloat16 [32, 4, 64, 256], P('dp', 'tile')
- gate_grad: float32 [32, 4, 4], P('dp', 'tile')
- kernel_grad: float32 [32, 9, 256, 256], P('dp', None, None, 'tile')
The draws below stay inside these ranges and needn't reach their ends.
Inputs may be any that keep to these rules, and one draw needn't show every extreme that they name: A tile's 4 experts have distinct values of id // 4. Among the 4 tiles of one device (frames d * 4 to (d + 1) * 4 - 1 at one tile index), each value of id // 4 is named by at most 2 tiles, by exactly 2 for some, and all its slots there name the same id. A tile uses its first counts slots; later slots are ignored.
All inputs are finite; a program needn't handle non-finite values.
Results may differ from the reference program's by a relative error of at most 0.005.
Values may be sent and summed in bfloat16 or wider, within the bound.
A program may use at most 256 MiB of HBM per device.

```python
import jax
import jax.numpy as jnp
from jax import lax

CHANNELS = 256
EXP_DEV = 4
SLOTS = 4
FR_DEV = 4
CAP = 2
TILE_ROWS = 1
TILE_COLS = 64
EXPERTS = 32
BATCH = 32
HEIGHT = 4
N_DP = 8
N_TILE = 4


def draw_experts(key, part):
    groups = N_DP * N_TILE
    listed = FR_DEV * SLOTS // CAP
    stride = SLOTS // CAP
    first, second, third, fourth = jax.random.split(key, 4)
    specialist_order = jax.random.permutation(first, N_DP)
    affinity_increment = jnp.maximum(0, 3 - specialist_order)
    stochastic_perturbation = jax.random.randint(second, (groups, N_DP), 0, 4)
    order_keys = jax.random.split(third, groups)
    equality_resolver = jax.vmap(lambda single: jax.random.permutation(single, N_DP))(order_keys)
    specialist_affinity = (stochastic_perturbation + affinity_increment[None, :]) * N_DP + equality_resolver
    listing = lax.top_k(specialist_affinity, listed)[1]
    spots = (jnp.arange(FR_DEV)[:, None] * stride + jnp.arange(SLOTS)[None, :]) % listed
    owners = listing[:, spots]
    local_ids = jax.random.randint(fourth, (groups, N_DP), 0, EXP_DEV)
    taken = jnp.take_along_axis(local_ids, owners.reshape(groups, FR_DEV * SLOTS), axis=1).reshape(owners.shape)
    ids = (owners * EXP_DEV + taken).astype(jnp.int32)
    ids = ids.reshape(N_DP, N_TILE, FR_DEV, SLOTS).transpose(0, 2, 1, 3)
    return ids.reshape(N_DP * FR_DEV, N_TILE, SLOTS)


def set_ends(values, own_key, smallest, high):
    place = [jax.random.randint(jax.random.fold_in(own_key, axis), (), 0, length) for axis, length in enumerate(values.shape)]
    main_axis = values.shape.index(max(values.shape))
    next_to = place[:main_axis] + [(place[main_axis] + 1) % values.shape[main_axis]] + place[main_axis + 1:]
    return values.at[tuple(place)].set(smallest).at[tuple(next_to)].set(high)


def levels(own_key, shape, cuts, smallest, top_value):
    factor_of = 1.0
    for dim, shards_of in cuts:
        draws = jax.random.uniform(jax.random.fold_in(jax.random.fold_in(own_key, 6), dim), (shards_of,), jnp.float32, smallest / len(cuts), top_value / len(cuts))
        factor_of = factor_of * jnp.repeat(jnp.exp(draws), shape[dim] // shards_of).reshape((-1,) + (1,) * (len(shape) - 1 - dim))
    return factor_of


def bell_draw(key, shape, spread, most, cuts=(), held_as=jnp.bfloat16):
    drawn = jax.random.normal(key, shape, jnp.float32) * spread
    if len(cuts) > 0:
        drawn = levels(key, shape, cuts, -0.22, 0.18) * drawn
    return jnp.clip(drawn, min=-most, max=most).astype(held_as)


def setup_inputs(seed: int = 0) -> dict:
    seeds = jax.random.split(jax.random.key(seed), 7)
    return {
        "frames": bell_draw(seeds[0], (BATCH, HEIGHT, TILE_COLS, CHANNELS), 1.0, 6.0, ((0, 8), (1, 4))),
        "kernels": bell_draw(seeds[1], (EXPERTS, 9, CHANNELS, CHANNELS), (9 * CHANNELS) ** -0.5, 0.125, ((0, 8),)),
        "experts": draw_experts(jax.random.fold_in(seeds[6], 71), 0),
        "counts": set_ends(jax.random.randint(seeds[3], (BATCH, N_TILE), 2, SLOTS + 1), jax.random.fold_in(seeds[3], 1), 2, SLOTS).astype(jnp.int32),
        "gate_weights": jnp.clip(0.25 + 0.75 * jax.random.uniform(seeds[4], (BATCH, N_TILE, SLOTS), jnp.float32) ** levels(seeds[4], (BATCH, N_TILE, SLOTS), ((0, 8), (1, 4)), -0.2, 0.2), 0.25, 1.0),
        "cotangent": bell_draw(seeds[5], (BATCH, HEIGHT, TILE_COLS, CHANNELS), 1.0, 6.0, ((0, 8), (1, 4))),
    }


def convolve(window, kernel_weight):
    number_of_rows = window.shape[0] - 2
    columns = window.shape[1]
    widened = jnp.pad(window, ((0, 0), (1, 1), (0, 0)))
    total = jnp.zeros((number_of_rows * columns, kernel_weight.shape[2]), jnp.float32)
    for row_off in range(3):
        for col_off in range(3):
            patch = widened[row_off:row_off + number_of_rows, col_off:col_off + columns].reshape(number_of_rows * columns, -1)
            total = total + jnp.dot(patch, kernel_weight[3 * row_off + col_off], preferred_element_type=jnp.float32)
    return total.reshape(number_of_rows, columns, -1)


def transpose_conv(grad_out, kernel_weight):
    number_of_rows = grad_out.shape[0]
    columns = grad_out.shape[1]
    widened = jnp.pad(grad_out, ((2, 2), (1, 1), (0, 0)))
    total = jnp.zeros(((number_of_rows + 2) * columns, kernel_weight.shape[1]), jnp.float32)
    for row_off in range(3):
        for col_off in range(3):
            patch = widened[2 - row_off:4 - row_off + number_of_rows, 2 - col_off:2 - col_off + columns].reshape((number_of_rows + 2) * columns, -1)
            total = total + lax.dot_general(patch, kernel_weight[3 * row_off + col_off], (((1,), (1,)), ((), ())), preferred_element_type=jnp.float32)
    return total.reshape(number_of_rows + 2, columns, -1)


def kernel_terms(window, grad_out):
    number_of_rows = grad_out.shape[0]
    columns = grad_out.shape[1]
    widened = jnp.pad(window, ((0, 0), (1, 1), (0, 0)))
    flat_grad = grad_out.reshape(number_of_rows * columns, -1)
    pieces = []
    for row_off in range(3):
        for col_off in range(3):
            patch = widened[row_off:row_off + number_of_rows, col_off:col_off + columns].reshape(number_of_rows * columns, -1)
            pieces.append(lax.dot_general(patch, flat_grad, (((0,), (0,)), ((), ())), preferred_element_type=jnp.float32))
    return jnp.stack(pieces)


def activation(pre):
    squash = jax.nn.sigmoid(pre)
    return pre * squash, squash * (1.0 + pre * (1.0 - squash))


def reference(frames, kernels, experts, counts, gate_weights, cotangent):
    padded_frames = jnp.pad(frames, ((0, 0), (1, 1), (0, 0), (0, 0)))
    width = frames.shape[2]
    channels = frames.shape[3]

    def advance(carry, index):
        kernel_grad, grad_frame = carry
        frame_index = index // N_TILE
        place_index = index % N_TILE
        first_row = (place_index * TILE_ROWS).astype(jnp.int32)
        anchor = jnp.zeros((), jnp.int32)
        window = lax.dynamic_slice(padded_frames, (frame_index, first_row, anchor, anchor), (1, TILE_ROWS + 2, width, channels))[0]
        upstream = lax.dynamic_slice(cotangent, (frame_index, first_row, anchor, anchor), (1, TILE_ROWS, width, channels))[0].astype(jnp.float32)
        chosen = experts[frame_index, place_index]
        active_count = counts[frame_index, place_index]
        gate_row = gate_weights[frame_index, place_index]
        result = window[1:-1].astype(jnp.float32)
        rim_sum = jnp.zeros((TILE_ROWS + 2, width, channels), jnp.float32)
        gate_terms = []
        for slot_index in range(SLOTS):
            kernel_weight = kernels[chosen[slot_index]]
            masked = (slot_index < active_count).astype(jnp.float32)
            gate_scale = masked * gate_row[slot_index].astype(jnp.float32)
            pre = lax.optimization_barrier(convolve(window, kernel_weight).astype(jnp.bfloat16)).astype(jnp.float32)
            activated, slope = activation(pre)
            result = result + gate_scale * activated
            gate_terms.append(masked * jnp.sum(upstream * activated))
            grad_pre = (upstream * gate_scale * slope).astype(jnp.bfloat16)
            kernel_grad = kernel_grad.at[chosen[slot_index]].add(kernel_terms(window, grad_pre))
            rim_sum = rim_sum + lax.optimization_barrier(transpose_conv(grad_pre, kernel_weight).astype(jnp.bfloat16)).astype(jnp.float32)
        former = lax.dynamic_slice(grad_frame, (frame_index, first_row, anchor, anchor), (1, TILE_ROWS + 2, width, channels))
        grad_frame = lax.dynamic_update_slice(grad_frame, former + rim_sum[None], (frame_index, first_row, anchor, anchor))
        return (kernel_grad, grad_frame), (result.astype(jnp.bfloat16), jnp.stack(gate_terms))

    initial = (jnp.zeros((kernels.shape[0], 9, channels, channels), jnp.float32),
               jnp.zeros((frames.shape[0], frames.shape[1] + 2, width, channels), jnp.float32))
    position_list = jnp.arange(frames.shape[0] * N_TILE, dtype=jnp.int32)
    (kernel_grad, grad_frame), (tiles, gate_terms) = lax.scan(advance, initial, position_list)
    tiles = tiles.reshape(frames.shape[0], N_TILE, TILE_ROWS, width, channels)
    frames_out = tiles.reshape(frames.shape)
    input_grad = (cotangent.astype(jnp.float32) + grad_frame[:, 1:-1]).astype(jnp.bfloat16)
    gate_grad = gate_terms.reshape(frames.shape[0], N_TILE, SLOTS)
    return (frames_out, input_grad, gate_grad, kernel_grad)
```

```python
import functools
from types import SimpleNamespace

import jax
import jax.numpy as jnp
from jax import lax
from jax.experimental import pallas as pl
from jax.experimental.pallas import tpu as pltpu
from jax.sharding import PartitionSpec as P

CAP = 2


def grid_of(owners):
    across = 1
    while across * across * 4 <= owners:
        across *= 2
    while owners % across:
        across -= 1
    return owners // across, across


def remote(src, dst, send, recv, dp, tile):
    return pltpu.make_async_remote_copy(
        src_ref=src,
        dst_ref=dst,
        send_sem=send,
        recv_sem=recv,
        device_id=(dp, tile),
        device_id_type=pl.DeviceIdType.MESH,
    )


def go(copy):
    copy.start()


def drain(copy):
    copy.wait_send()


def layer_kernel(
    deep, across, high, cores, names,
    frames_ref, cot_ref, note_ref, weight_ref, bank_hbm,
    result_ref, input_ref, gated_ref, grad_ref, *rest,
):
    v = SimpleNamespace(**dict(zip(names, rest)))
    me, t = lax.axis_index("dp"), lax.axis_index("tile")
    z, x = me // across, me % across
    y, core = t // cores, t % cores
    owners, tiles = deep * across, high * cores
    frames, columns, channels = frames_ref.shape
    experts, taps, share, _ = grad_ref.shape
    cap = CAP
    rows = cap * columns
    has_above, has_below = t > 0, t < tiles - 1
    t_above, t_below = (t + tiles - 1) % tiles, (t + 1) % tiles
    bf16, f32 = jnp.bfloat16, jnp.float32

    load_bank = pltpu.make_async_copy(bank_hbm, v.bank, v.local_sem.at[0])
    load_bank.start()

    barrier = pltpu.get_barrier_semaphore()
    for j in range(1, owners):
        pl.semaphore_signal(
            barrier, device_id=((me + j) % owners, t), device_id_type=pl.DeviceIdType.MESH
        )
    for j in range(1, tiles):
        pl.semaphore_signal(
            barrier, device_id=(me, (t + j) % tiles), device_id_type=pl.DeviceIdType.MESH
        )
    pl.semaphore_wait(barrier, owners - 1 + tiles - 1)

    def lift(act, s, fr, co):
        act(remote(fr, v.f.at[s, t], v.f_up.at[s], v.f_recv.at[s], me + across, t))
        act(remote(co, v.c.at[s], v.c_up.at[s], v.c_recv.at[s], me + across, t))

    def sink(act, s, fr, co):
        act(remote(fr, v.f.at[s, t], v.f_down.at[s], v.f_recv.at[s], me - across, t))
        act(remote(co, v.c.at[s], v.c_down.at[s], v.c_recv.at[s], me - across, t))

    def side_frames(act, s, fr):
        for j in range(1, across):
            act(
                remote(
                    fr, v.f.at[s, t], v.f_side.at[j - 1, s], v.f_recv.at[s],
                    z * across + (x + j) % across, t,
                )
            )

    def side_packed(act, s, zs):
        for j in range(1, across):
            act(
                remote(
                    v.cpo.at[j - 1, zs], v.cp.at[s], v.cp_send.at[j - 1, zs], v.cp_recv.at[s],
                    z * across + (x + j) % across, t,
                )
            )

    def tile_frames(act, s, fr):
        for j in range(1, cores):
            act(
                remote(
                    fr, v.f.at[s, t], v.mate_send.at[j - 1, s], v.ft_recv.at[s, t],
                    me, y * cores + (core + j) % cores,
                )
            )
        for j in range(1, high):
            act(
                remote(
                    fr, v.f.at[s, t], v.far_tile.at[j - 1, s], v.ft_recv.at[s, t],
                    me, (y + j) % high * cores + core,
                )
            )

    def pass_on(act, s, j):
        tt = (y + j) % high * cores + core
        for i in range(1, cores):
            act(
                remote(
                    v.f.at[s, tt], v.f.at[s, tt], v.pass_send.at[j - 1, i - 1, s],
                    v.ft_recv.at[s, tt], me, y * cores + (core + i) % cores,
                )
            )

    def edge_down(act, s):
        act(
            remote(
                v.eo.at[s, 1], v.above.at[s], v.above_send.at[s], v.above_recv.at[s], me, t + 1
            )
        )

    def edge_up(act, s):
        act(
            remote(
                v.eo.at[s, 0], v.below.at[s], v.below_send.at[s], v.below_recv.at[s], me, t - 1
            )
        )

    def slices(act, s):
        for j in range(1, tiles):
            tt = (t + j) % tiles
            act(
                remote(
                    v.go.at[s, tt], v.gi.at[s, t], v.g_send.at[j - 1, s], v.g_recv.at[s, t], me, tt
                )
            )

    def gates(act, s):
        act(
            remote(
                v.gate.at[s], gated_ref.at[me], v.gate_send.at[s], v.gate_recv.at[me], s, t
            )
        )

    def side_terms(act, s, zs, xj):
        act(
            remote(
                v.sbo.at[xj - 1, zs], v.sbi.at[xj - 1, zs],
                v.sb_send.at[xj - 1, zs], v.sb_recv.at[xj - 1, zs], z * across + s % across, t,
            )
        )
        act(
            remote(
                v.act.at[s], v.sai.at[xj - 1, zs],
                v.sa_send.at[xj - 1, zs], v.sa_recv.at[xj - 1, zs], z * across + s % across, t,
            )
        )

    def far_terms(act, zs):
        act(
            remote(
                v.fo.at[zs], v.fi.at[z], v.fo_send.at[zs], v.fi_recv.at[z], zs * across + x, t
            )
        )

    def received(ref, sem):
        remote(ref, ref, v.spare_sem.at[0], sem, me, t).wait_recv()

    def send_notes(act):
        for j in range(1, owners):
            peer = (me + j) % owners
            act(
                remote(
                    note_ref.at[pl.ds(peer // across * across, across)], v.n.at[me],
                    v.note_send.at[0, j - 1], v.note_recv.at[0, me], peer, t,
                )
            )
            act(
                remote(
                    weight_ref.at[peer], v.w.at[me],
                    v.note_send.at[1, j - 1], v.note_recv.at[1, me], peer, t,
                )
            )

    send_notes(go)
    own_notes = pltpu.make_async_copy(
        note_ref.at[pl.ds(z * across, across)], v.n.at[me], v.local_sem.at[1]
    )
    own_notes.start()
    own_weights = pltpu.make_async_copy(weight_ref.at[me], v.w.at[me], v.local_sem.at[2])
    own_weights.start()
    own_rows = pltpu.make_async_copy(frames_ref, v.f.at[me, t], v.local_sem.at[3])
    own_rows.start()
    pl.when(z < deep - 1)(lambda: lift(go, me, frames_ref, cot_ref))
    pl.when(z > 0)(lambda: sink(go, me, frames_ref, cot_ref))
    side_frames(go, me, frames_ref)
    tile_frames(go, me, frames_ref)

    @pl.when(jnp.logical_not(has_above))
    def _():
        v.above[...] = jnp.zeros_like(v.above)

    @pl.when(jnp.logical_not(has_below))
    def _():
        v.below[...] = jnp.zeros_like(v.below)

    own_notes.wait()
    own_weights.wait()
    for j in range(1, owners):
        s = (me + j) % owners
        received(v.n.at[s], v.note_recv.at[0, s])
        received(v.w.at[s], v.note_recv.at[1, s])

    def tile_notes(act):
        for j in range(1, tiles):
            act(
                remote(
                    v.n, v.tn.at[t], v.tn_send.at[j - 1], v.tn_recv.at[t], me, (t + j) % tiles
                )
            )

    tile_notes(go)
    copies = [
        pltpu.make_async_copy(v.n, v.tn.at[t], v.local_sem.at[1]),
        pltpu.make_async_copy(v.n, v.ns, v.local_sem.at[2]),
        pltpu.make_async_copy(v.w, v.ws, v.local_sem.at[4]),
    ]
    for copy in copies:
        copy.start()
    for copy in copies:
        copy.wait()

    def places(s, xo):
        return [v.ns[s, xo, 0, 1 + c] for c in range(cap)]

    def tile_places(tt, s):
        return [v.ts[tt, s, x, 0, 1 + c] for c in range(cap)]

    def picked(spots, load):
        parts = []
        for c in range(cap):
            value = jnp.zeros((columns, channels), bf16)
            for f in range(frames):
                value = jnp.where(spots[c] == f, load(f), value)
            parts.append(value)
        return parts

    def pack(s, zs, load):
        for j in range(1, across):
            parts = picked(places(s, (x + j) % across), load)
            for c in range(cap):
                v.cpo[j - 1, zs, c] = parts[c]
        parts = picked(places(s, x), load)
        for c in range(cap):
            v.cp[s, c] = parts[c]
        side_packed(go, s, zs)

    pack(me, z, lambda f: cot_ref[f])

    for j in range(1, tiles):
        tt = (t + j) % tiles
        received(v.tn.at[tt], v.tn_recv.at[tt])
    tile_scalars = pltpu.make_async_copy(v.tn, v.ts, v.local_sem.at[1])
    tile_scalars.start()
    tile_scalars.wait()
    own_rows.wait()
    load_bank.wait()

    count = (2 * deep - 1) * across

    def stage(n, body, lead=None):
        j, xj = n // across, n % across
        zs = z + (j + 1) // 2 * (1 - 2 * (j % 2))
        s = zs * across + (x + xj) % across
        cond = jnp.logical_and(
            jnp.logical_and(n >= 0, n < count), jnp.logical_and(zs >= 0, zs < deep)
        )
        if lead is True:
            cond = jnp.logical_and(cond, xj == 0)
        elif lead is False:
            cond = jnp.logical_and(cond, xj > 0)
        pl.when(cond)(lambda: body(s, zs, xj))

    def arrive(s, zs, xj):
        received(v.f.at[s, t], v.f_recv.at[s])

        @pl.when(xj == 0)
        def _():
            received(v.c.at[s], v.c_recv.at[s])
            pl.when(jnp.logical_and(zs < z, z < deep - 1))(
                lambda: lift(go, s, v.f.at[s, t], v.c.at[s])
            )
            pl.when(jnp.logical_and(zs > z, z > 0))(
                lambda: sink(go, s, v.f.at[s, t], v.c.at[s])
            )
            side_frames(go, s, v.f.at[s, t])
            pack(s, zs, lambda f: v.c[s, f])

        @pl.when(xj > 0)
        def _():
            received(v.cp.at[s], v.cp_recv.at[s])

        tile_frames(go, s, v.f.at[s, t])

    def across_tiles(s, zs, xj):
        for j in range(1, high):
            tt = (y + j) % high * cores + core
            received(v.f.at[s, tt], v.ft_recv.at[s, tt])
            pass_on(go, s, j)

    place = lax.broadcasted_iota(jnp.int32, (rows, 1), 0)
    item = place // columns
    column = place % columns

    def later(value):
        return jnp.where(column == 0, 0.0, pltpu.roll(value, 1, 0))

    def sooner(value):
        return jnp.where(column == columns - 1, 0.0, pltpu.roll(value, rows - 1, 0))

    def compute(s, zs, xj):
        for j in range(high):
            for i in range(1, cores):
                tt = (y + j) % high * cores + (core + i) % cores
                received(v.f.at[s, tt], v.ft_recv.at[s, tt])
        e = v.ns[s, x, 0, 0]
        spots = places(s, x)
        blank = jnp.zeros((rows, channels), bf16)

        def gather(tt):
            return jnp.concatenate(picked(spots, lambda f: v.f[s, tt, f]), axis=0)

        window = [
            jnp.where(has_above, gather(t_above), blank),
            gather(t),
            jnp.where(has_below, gather(t_below), blank),
        ]
        upstream = v.cp[s].reshape(rows, channels).astype(f32)
        weight = jnp.zeros((rows, 1), f32)
        for c in range(cap):
            weight = jnp.where(item == c, v.ws[s, 0, c], weight)

        def column_term(db):
            total = jnp.dot(window[0], v.bank[e, db], preferred_element_type=f32)
            for da in (1, 2):
                total = total + jnp.dot(
                    window[da], v.bank[e, 3 * da + db], preferred_element_type=f32
                )
            return total

        pre = column_term(1) + later(column_term(0)) + sooner(column_term(2))
        pre = pre.astype(bf16).astype(f32)
        squash = jax.nn.sigmoid(pre)
        activated = pre * squash
        slope = squash * (1.0 + pre * (1.0 - squash))
        v.act[s] = (weight * activated).astype(bf16).reshape(cap, columns, channels)
        sums = jnp.sum((upstream * activated).reshape(cap, columns, channels), axis=1)
        sums = jnp.broadcast_to(jnp.sum(sums, axis=1, keepdims=True), (cap, 128))
        sums = jnp.concatenate([sums, jnp.zeros((8 - cap, 128), f32)], axis=0)
        v.gate[s] = sums

        @pl.when(s != me)
        def _():
            gates(go, s)

        @pl.when(s == me)
        def _():
            gated_ref[me] = sums

        grad = (upstream * weight * slope).astype(bf16)
        turned = jnp.transpose(grad.astype(f32)).astype(bf16)
        for k in range(tiles):
            v.go[s, k] = turned[k * share : (k + 1) * share]
        v.gi[s, t] = v.go[s, t]
        slices(go, s)
        for da in (0, 2, 1):
            parts = [
                lax.dot_general(
                    grad,
                    v.bank[e, 3 * da + db],
                    (((1,), (1,)), ((), ())),
                    preferred_element_type=f32,
                )
                for db in range(3)
            ]
            total = parts[1] + sooner(parts[0]) + later(parts[2])
            total = total.astype(bf16).reshape(cap, columns, channels)
            if da == 1:
                v.bk[s] = total
            else:
                v.eo[s, da // 2] = total
        pl.when(has_above)(lambda: edge_up(go, s))
        pl.when(has_below)(lambda: edge_down(go, s))

    def rims(s):
        pl.when(has_above)(lambda: received(v.above.at[s], v.above_recv.at[s]))
        pl.when(has_below)(lambda: received(v.below.at[s], v.below_recv.at[s]))

    def spread_out(value, spots, load, f):
        for c in range(cap):
            value = value + jnp.where(spots[c] == f, load(c).astype(f32), 0.0)
        return value

    def back_rows(s):
        mine = places(s, x)
        upper = [jnp.where(has_above, p, -1) for p in tile_places(t_above, s)]
        lower = [jnp.where(has_below, p, -1) for p in tile_places(t_below, s)]

        def row(f):
            value = jnp.zeros((columns, channels), f32)
            value = spread_out(value, mine, lambda c: v.bk[s, c], f)
            value = spread_out(value, upper, lambda c: v.above[s, c], f)
            return spread_out(value, lower, lambda c: v.below[s, c], f)

        return row

    def to_side(s, zs, xj):
        rims(s)
        row = back_rows(s)
        for f in range(frames):
            v.sbo[xj - 1, zs, f] = row(f).astype(bf16)
        side_terms(go, s, zs, xj)

    def to_far(s, zs, xj):
        rims(s)
        for j in range(1, across):
            received(v.sbi.at[j - 1, zs], v.sb_recv.at[j - 1, zs])
            received(v.sai.at[j - 1, zs], v.sa_recv.at[j - 1, zs])
        row = back_rows(s)
        spots = [places(s, x)] + [places(s, (x + across - j) % across) for j in range(1, across)]
        for f in range(frames):
            first = row(f)
            second = spread_out(
                jnp.zeros((columns, channels), f32), spots[0], lambda c: v.act[s, c], f
            )
            for j in range(1, across):
                first = first + v.sbi[j - 1, zs, f].astype(f32)
                second = spread_out(second, spots[j], lambda c: v.sai[j - 1, zs, c], f)
            v.total[0, f] = first
            v.total[1, f] = second

        @pl.when(zs == z)
        def _():
            for f in range(frames):
                v.base[0, f] = v.total[0, f] + cot_ref[f].astype(f32)
                v.base[1, f] = v.total[1, f] + frames_ref[f].astype(f32)

        @pl.when(zs != z)
        def _():
            v.fo[zs] = v.total[...].astype(bf16)
            far_terms(go, zs)

    @pl.loop(0, count + across + 3)
    def _(n):
        stage(n - 2, compute)
        stage(n - 3, to_side, lead=False)
        stage(n - across - 3, to_far, lead=True)
        stage(n - 1, across_tiles)
        pl.when(n > 0)(lambda: stage(n, arrive))

    @pl.loop(0, experts)
    def _(k):
        grad_ref[k] = jnp.zeros_like(grad_ref[k])

    lane = lax.broadcasted_iota(jnp.int32, (1, rows), 1) % columns

    @pl.loop(0, owners)
    def _(i):
        s = (me + i) % owners
        for j in range(1, tiles):
            tt = (t + j) % tiles
            received(v.gi.at[s, tt], v.g_recv.at[s, tt])
        for tt in range(tiles):
            e = v.ts[tt, s, x, 0, 0]
            spots = tile_places(tt, s)
            span = slice(tt * rows, (tt + 1) * rows)
            for da in range(3):
                source = tt + da - 1
                if 0 <= source < tiles:
                    parts = picked(spots, lambda f: v.f[s, source, f])
                    v.xw[da, span] = jnp.concatenate(parts, axis=0)
                else:
                    v.xw[da, span] = jnp.zeros((rows, channels), bf16)
            g = v.gi[s, tt].astype(f32)
            moved = [
                jnp.where(lane == columns - 1, 0.0, pltpu.roll(g, rows - 1, 1)).astype(bf16),
                v.gi[s, tt],
                jnp.where(lane == 0, 0.0, pltpu.roll(g, 1, 1)).astype(bf16),
            ]
            for db in range(3):
                for k in range(experts):
                    v.gt[db, k * share : (k + 1) * share, span] = jnp.where(
                        e == k, moved[db], jnp.zeros_like(moved[db])
                    )
        for da in range(3):
            for db in range(3):
                term = jnp.dot(v.gt[db], v.xw[da], preferred_element_type=f32)
                grad_ref[:, 3 * da + db] += term.reshape(experts, share, channels)

    for k in range(1, deep):
        zs = (z + k) % deep
        received(v.fi.at[zs], v.fi_recv.at[zs])
    for f in range(frames):
        first, second = v.base[0, f], v.base[1, f]
        for k in range(1, deep):
            zs = (z + k) % deep
            first = first + v.fi[zs, 0, f].astype(f32)
            second = second + v.fi[zs, 1, f].astype(f32)
        input_ref[f] = first.astype(bf16)
        result_ref[f] = second.astype(bf16)

    for j in range(1, owners):
        s = (me + j) % owners
        received(gated_ref.at[s], v.gate_recv.at[s])
        gates(drain, s)
    send_notes(drain)
    tile_notes(drain)
    pl.when(z < deep - 1)(lambda: lift(drain, me, frames_ref, cot_ref))
    pl.when(z > 0)(lambda: sink(drain, me, frames_ref, cot_ref))

    def finish(s, zs, xj):
        @pl.when(xj == 0)
        def _():
            pl.when(jnp.logical_and(zs < z, z < deep - 1))(
                lambda: lift(drain, s, v.f.at[s, t], v.c.at[s])
            )
            pl.when(jnp.logical_and(zs > z, z > 0))(
                lambda: sink(drain, s, v.f.at[s, t], v.c.at[s])
            )
            side_frames(drain, s, v.f.at[s, t])
            side_packed(drain, s, zs)
            pl.when(zs != z)(lambda: far_terms(drain, zs))

        pl.when(xj > 0)(lambda: side_terms(drain, s, zs, xj))
        tile_frames(drain, s, v.f.at[s, t])
        for j in range(1, high):
            pass_on(drain, s, j)
        slices(drain, s)
        pl.when(has_above)(lambda: edge_up(drain, s))
        pl.when(has_below)(lambda: edge_down(drain, s))

    @pl.loop(0, count)
    def _(n):
        stage(n, finish)


def layer(frames, cot, note, weight, kernels, owners, tiles):
    deep, across = grid_of(owners)
    cores = 1 if tiles % 2 else 2
    high = tiles // cores
    count, columns, channels = frames.shape
    experts, taps, _, outputs = kernels.shape
    share = outputs // tiles
    cap = CAP
    rows = cap * columns
    dma = pltpu.SemaphoreType.DMA
    vmem = pl.BlockSpec(memory_space=pltpu.VMEM)
    bf16, f32, i32 = jnp.bfloat16, jnp.float32, jnp.int32
    beside, mates, far = (max(value - 1, 1) for value in (across, cores, high))
    others, peers = max(owners - 1, 1), max(tiles - 1, 1)
    scratch = dict(
        f=pltpu.VMEM((owners, tiles, count, columns, channels), bf16),
        c=pltpu.VMEM((owners, count, columns, channels), bf16),
        cp=pltpu.VMEM((owners, cap, columns, channels), bf16),
        cpo=pltpu.VMEM((beside, deep, cap, columns, channels), bf16),
        n=pltpu.VMEM((owners, across, 1, 128), i32),
        w=pltpu.VMEM((owners, 1, 128), f32),
        tn=pltpu.VMEM((tiles, owners, across, 1, 128), i32),
        ns=pltpu.SMEM((owners, across, 1, 128), i32),
        ws=pltpu.SMEM((owners, 1, 128), f32),
        ts=pltpu.SMEM((tiles, owners, across, 1, 128), i32),
        bank=pltpu.VMEM(kernels.shape, bf16),
        act=pltpu.VMEM((owners, cap, columns, channels), bf16),
        bk=pltpu.VMEM((owners, cap, columns, channels), bf16),
        eo=pltpu.VMEM((owners, 2, cap, columns, channels), bf16),
        above=pltpu.VMEM((owners, cap, columns, channels), bf16),
        below=pltpu.VMEM((owners, cap, columns, channels), bf16),
        go=pltpu.VMEM((owners, tiles, share, rows), bf16),
        gi=pltpu.VMEM((owners, tiles, share, rows), bf16),
        gate=pltpu.VMEM((owners, 8, 128), f32),
        sbo=pltpu.VMEM((beside, deep, count, columns, channels), bf16),
        sbi=pltpu.VMEM((beside, deep, count, columns, channels), bf16),
        sai=pltpu.VMEM((beside, deep, cap, columns, channels), bf16),
        fo=pltpu.VMEM((deep, 2, count, columns, channels), bf16),
        fi=pltpu.VMEM((deep, 2, count, columns, channels), bf16),
        total=pltpu.VMEM((2, count, columns, channels), f32),
        base=pltpu.VMEM((2, count, columns, channels), f32),
        xw=pltpu.VMEM((3, tiles * rows, channels), bf16),
        gt=pltpu.VMEM((3, experts * share, tiles * rows), bf16),
        local_sem=dma((5,)),
        spare_sem=dma((1,)),
        note_send=dma((2, others)), note_recv=dma((2, owners)),
        tn_send=dma((peers,)), tn_recv=dma((tiles,)),
        f_up=dma((owners,)), f_down=dma((owners,)), f_side=dma((beside, owners)), f_recv=dma((owners,)),
        c_up=dma((owners,)), c_down=dma((owners,)), c_recv=dma((owners,)),
        cp_send=dma((beside, deep)), cp_recv=dma((owners,)),
        mate_send=dma((mates, owners)), far_tile=dma((far, owners)),
        pass_send=dma((far, mates, owners)), ft_recv=dma((owners, tiles)),
        above_send=dma((owners,)), above_recv=dma((owners,)),
        below_send=dma((owners,)), below_recv=dma((owners,)),
        g_send=dma((peers, owners)), g_recv=dma((owners, tiles)),
        gate_send=dma((owners,)), gate_recv=dma((owners,)),
        sb_send=dma((beside, deep)), sb_recv=dma((beside, deep)),
        sa_send=dma((beside, deep)), sa_recv=dma((beside, deep)),
        fo_send=dma((deep,)), fi_recv=dma((deep,)),
    )
    return pl.pallas_call(
        functools.partial(layer_kernel, deep, across, high, cores, tuple(scratch)),
        out_shape=[
            jax.ShapeDtypeStruct(frames.shape, bf16),
            jax.ShapeDtypeStruct(frames.shape, bf16),
            jax.ShapeDtypeStruct((owners, 8, 128), f32),
            jax.ShapeDtypeStruct((experts, taps, share, channels), f32),
        ],
        in_specs=[vmem] * 4 + [pl.BlockSpec(memory_space=pl.ANY)],
        out_specs=[vmem] * 4,
        scratch_shapes=list(scratch.values()),
        compiler_params=pltpu.CompilerParams(
            collective_id=0, has_side_effects=True, vmem_limit_bytes=58 * 1024 * 1024
        ),
        name="layer",
    )(frames, cot, note, weight, kernels)


def shards(frames, kernels, experts, counts, gate_weights, cotangent):
    owners = lax.axis_size("dp")
    tiles = lax.axis_size("tile")
    local = kernels.shape[0]
    chosen = experts[:, 0]
    frame_count, slots = chosen.shape
    active = jnp.arange(slots)[None, :] < counts[:, 0][:, None]
    owner_of = chosen // local
    hit = (owner_of[:, :, None] == jnp.arange(owners)) & active[:, :, None]
    wanted = jnp.any(hit, axis=1)
    position = jnp.cumsum(wanted.astype(jnp.int32), axis=0) - 1
    slot_map = wanted.T[:, None, :] & (
        position.T[:, None, :] == jnp.arange(CAP)[None, :, None]
    )
    request = jnp.max(jnp.where(hit, (chosen % local)[:, :, None], 0), axis=(0, 1))
    tile_gate = jnp.sum(jnp.where(hit, gate_weights[:, 0][:, :, None], 0.0), axis=1)
    weight = jnp.sum(jnp.where(slot_map, tile_gate.T[:, None, :], 0.0), axis=2)
    place = jnp.sum(
        jnp.where(slot_map, jnp.arange(1, frame_count + 1)[None, None, :], 0), axis=2
    ) - 1
    note = jnp.concatenate([request[:, None], place], axis=1).astype(jnp.int32)
    note = jnp.pad(note[:, None, :], ((0, 0), (0, 0), (0, 128 - note.shape[1])))
    weight = jnp.pad(weight[:, None, :], ((0, 0), (0, 0), (0, 128 - CAP)))
    result, input_grad, gated, kernel_part = layer(
        frames[:, 0], cotangent[:, 0], note, weight, kernels, owners, tiles
    )
    kernel_part = jnp.swapaxes(kernel_part, 2, 3)
    gated = gated[:, :CAP, 0]
    selected = jnp.sum(jnp.where(slot_map, gated[:, :, None], 0.0), axis=1)
    gate_grad = jnp.sum(jnp.where(hit, selected.T[:, None, :], 0.0), axis=2)
    return (result[:, None], input_grad[:, None], gate_grad[:, None, :], kernel_part)


def solution(mesh):
    return jax.shard_map(
        shards,
        mesh=mesh,
        in_specs=(
            P("dp", "tile", None, None),
            P("dp", None, None, None),
            P("dp", "tile", None),
            P("dp", "tile"),
            P("dp", "tile", None),
            P("dp", "tile", None, None),
        ),
        out_specs=(
            P("dp", "tile", None, None),
            P("dp", "tile", None, None),
            P("dp", "tile", None),
            P("dp", None, None, "tile"),
        ),
        check_vma=False,
    )
```

```python
import functools
import math
from types import SimpleNamespace

import jax
import jax.numpy as jnp
from jax import lax
from jax.experimental import pallas as pl
from jax.experimental.pallas import tpu as pltpu
from jax.sharding import PartitionSpec as P

CAP = 2


def grid_of(owners):
    across = 1
    while across * across * 4 <= owners:
        across *= 2
    while owners % across:
        across -= 1
    return owners // across, across


def remote(src, dst, send, recv, dp, tile):
    return pltpu.make_async_remote_copy(
        src_ref=src,
        dst_ref=dst,
        send_sem=send,
        recv_sem=recv,
        device_id=(dp, tile),
        device_id_type=pl.DeviceIdType.MESH,
    )


def go(copy):
    copy.start()


def drain(copy):
    copy.wait_send()


def layer_kernel(
    deep, across, high, cores, names,
    frames_hbm, cot_hbm, note_ref, weight_ref, bank_hbm,
    result_ref, input_ref, gated_ref, grad_ref, *rest,
):
    v = SimpleNamespace(**dict(zip(names, rest)))
    me, t = lax.axis_index("dp"), lax.axis_index("tile")
    z, x = me // across, me % across
    y, core = t // cores, t % cores
    owners, tiles = deep * across, high * cores
    _, _, frames, columns, channels = v.f.shape
    experts, taps, share, _ = grad_ref.shape
    cap = CAP
    rows = cap * columns
    has_above, has_below = t > 0, t < tiles - 1
    t_above, t_below = (t + tiles - 1) % tiles, (t + 1) % tiles
    bf16, f32 = jnp.bfloat16, jnp.float32

    load_bank = pltpu.make_async_copy(bank_hbm, v.bank, v.local_sem.at[0])
    own_rows = pltpu.make_async_copy(frames_hbm, v.f.at[me, t], v.local_sem.at[3])
    own_rows.start()
    own_cot = pltpu.make_async_copy(cot_hbm, v.c.at[me], v.local_sem.at[5])
    own_cot.start()
    load_bank.start()
    own_scalars = pltpu.make_async_copy(note_ref, v.os, v.local_sem.at[4])
    own_scalars.start()

    barrier = pltpu.get_barrier_semaphore()
    for j in range(1, owners):
        pl.semaphore_signal(
            barrier, device_id=((me + j) % owners, t), device_id_type=pl.DeviceIdType.MESH
        )
    for j in range(1, tiles):
        pl.semaphore_signal(
            barrier, device_id=(me, (t + j) % tiles), device_id_type=pl.DeviceIdType.MESH
        )
    pl.semaphore_wait(barrier, owners - 1 + tiles - 1)

    def along(act, s, zs, fr, co):
        up = jnp.logical_and(zs <= z, z < deep - 1)
        down = jnp.logical_and(zs >= z, z > 0)
        if fr is not None:
            pl.when(up)(
                lambda: act(
                    remote(fr, v.f.at[s, t], v.f_up.at[s], v.f_recv.at[s], me + across, t)
                )
            )
            pl.when(down)(
                lambda: act(
                    remote(fr, v.f.at[s, t], v.f_down.at[s], v.f_recv.at[s], me - across, t)
                )
            )
        if co is not None:
            pl.when(up)(
                lambda: act(remote(co, v.c.at[s], v.c_up.at[s], v.c_recv.at[s], me + across, t))
            )
            pl.when(down)(
                lambda: act(remote(co, v.c.at[s], v.c_down.at[s], v.c_recv.at[s], me - across, t))
            )

    def side_frames(act, s, fr):
        for j in range(1, across):
            act(
                remote(
                    fr, v.f.at[s, t], v.f_side.at[j - 1, s], v.f_recv.at[s],
                    z * across + (x + j) % across, t,
                )
            )

    def side_packed(act, s, zs):
        for j in range(1, across):
            act(
                remote(
                    v.cpo.at[j - 1, zs], v.cp.at[s], v.cp_send.at[j - 1, zs], v.cp_recv.at[s],
                    z * across + (x + j) % across, t,
                )
            )

    def near_rows(act, s, fr):
        pl.when(has_below)(
            lambda: act(
                remote(fr, v.f.at[s, t], v.near_send.at[0, s], v.ft_recv.at[s, t], me, t + 1)
            )
        )
        pl.when(has_above)(
            lambda: act(
                remote(fr, v.f.at[s, t], v.near_send.at[1, s], v.ft_recv.at[s, t], me, t - 1)
            )
        )

    def far_rows(act, s):
        for j in range(1, high):
            yy = (y + j) % high
            beside = jnp.logical_or(
                jnp.logical_and(yy == y + 1, core == cores - 1),
                jnp.logical_and(yy == y - 1, core == 0),
            )
            pl.when(jnp.logical_not(beside))(
                lambda j=j, yy=yy: act(
                    remote(
                        v.f.at[s, t], v.f.at[s, t], v.far_send.at[j - 1, s], v.ft_recv.at[s, t],
                        me, yy * cores + core,
                    )
                )
            )

    def entering(body):
        for j in range(1, high):
            yy = (y + j) % high
            for c in range(cores):
                across_low = jnp.logical_and(yy == y - 1, c == cores - 1)
                across_high = jnp.logical_and(yy == y + 1, c == 0)
                straight = jnp.logical_not(jnp.logical_or(across_low, across_high))
                enters = jnp.logical_or(
                    jnp.logical_and(across_low, core == 0),
                    jnp.logical_or(
                        jnp.logical_and(across_high, core == cores - 1),
                        jnp.logical_and(straight, core == c),
                    ),
                )
                body(j, c, yy * cores + c, enters, straight)

    def pass_on(act, s):
        def one(j, c, tt, enters, straight):
            @pl.when(enters)
            def _():
                for i in range(1, cores):
                    act(
                        remote(
                            v.f.at[s, tt], v.f.at[s, tt], v.pass_send.at[j - 1, c, i - 1, s],
                            v.ft_recv.at[s, tt], me, y * cores + (core + i) % cores,
                        )
                    )

        entering(one)

    def gather_far(s):
        def one(j, c, tt, enters, straight):
            pl.when(jnp.logical_and(enters, straight))(
                lambda: received(v.f.at[s, tt], v.ft_recv.at[s, tt])
            )

        entering(one)
        pass_on(go, s)

    def gather_passed(s):
        def one(j, c, tt, enters, straight):
            pl.when(jnp.logical_not(enters))(
                lambda: received(v.f.at[s, tt], v.ft_recv.at[s, tt])
            )

        entering(one)

    def edge_down(act, s):
        act(
            remote(
                v.eo.at[s, 1], v.above.at[s], v.above_send.at[s], v.above_recv.at[s], me, t + 1
            )
        )

    def edge_up(act, s):
        act(
            remote(
                v.eo.at[s, 0], v.below.at[s], v.below_send.at[s], v.below_recv.at[s], me, t - 1
            )
        )

    def slices(act, s):
        for j in range(1, tiles):
            tt = (t + j) % tiles
            act(
                remote(
                    v.go.at[s, tt], v.gi.at[s, t], v.g_send.at[j - 1, s], v.g_recv.at[s, t], me, tt
                )
            )

    def gates(act, s):
        act(
            remote(
                v.gate.at[s], gated_ref.at[me], v.gate_send.at[s], v.gate_recv.at[me], s, t
            )
        )

    def side_terms(act, s, zs, xj):
        act(
            remote(
                v.sbo.at[xj - 1, zs], v.sbi.at[xj - 1, zs],
                v.sb_send.at[xj - 1, zs], v.sb_recv.at[xj - 1, zs], z * across + s % across, t,
            )
        )
        act(
            remote(
                v.act.at[s], v.sai.at[xj - 1, zs],
                v.sa_send.at[xj - 1, zs], v.sa_recv.at[xj - 1, zs], z * across + s % across, t,
            )
        )

    def far_terms(act, zs):
        act(
            remote(
                v.fo.at[zs], v.fi.at[z], v.fo_send.at[zs], v.fi_recv.at[z], zs * across + x, t
            )
        )

    def received(ref, sem):
        remote(ref, ref, v.spare_sem.at[0], sem, me, t).wait_recv()

    def send_notes(act):
        for j in range(1, owners):
            peer = (me + j) % owners
            act(
                remote(
                    note_ref.at[pl.ds(peer // across * across, across)], v.n.at[me],
                    v.note_send.at[0, j - 1], v.note_recv.at[0, me], peer, t,
                )
            )
            act(
                remote(
                    weight_ref.at[peer], v.w.at[me],
                    v.note_send.at[1, j - 1], v.note_recv.at[1, me], peer, t,
                )
            )

    send_notes(go)
    own_notes = pltpu.make_async_copy(
        note_ref.at[pl.ds(z * across, across)], v.n.at[me], v.local_sem.at[1]
    )
    own_notes.start()
    own_weights = pltpu.make_async_copy(weight_ref.at[me], v.w.at[me], v.local_sem.at[2])
    own_weights.start()
    own_rows.wait()
    along(go, me, z, v.f.at[me, t], None)
    side_frames(go, me, v.f.at[me, t])
    near_rows(go, me, v.f.at[me, t])
    own_cot.wait()
    along(go, me, z, None, v.c.at[me])

    def places(s, xo):
        return [v.ns[s, xo, 0, 1 + c] for c in range(cap)]

    def tile_places(tt, s):
        return [v.ts[tt, s, x, 0, 1 + c] for c in range(cap)]

    def picked(spots, load):
        parts = []
        for c in range(cap):
            value = jnp.zeros((columns, channels), bf16)
            for f in range(frames):
                value = jnp.where(spots[c] == f, load(f), value)
            parts.append(value)
        return parts

    def pack(s, zs, load, spots_of):
        for j in range(1, across):
            parts = picked(spots_of((x + j) % across), load)
            for c in range(cap):
                v.cpo[j - 1, zs, c] = parts[c]
        side_packed(go, s, zs)
        parts = picked(spots_of(x), load)
        for c in range(cap):
            v.cp[s, c] = parts[c]

    own_scalars.wait()
    pack(
        me, z, lambda f: v.c[me, f],
        lambda xo: [v.os[z * across + xo, 0, 1 + c] for c in range(cap)],
    )

    @pl.when(jnp.logical_not(has_above))
    def _():
        v.above[...] = jnp.zeros_like(v.above)

    @pl.when(jnp.logical_not(has_below))
    def _():
        v.below[...] = jnp.zeros_like(v.below)

    @pl.loop(0, experts)
    def _(k):
        grad_ref[k] = jnp.zeros_like(grad_ref[k])

    def tile_notes(act):
        for j in range(1, tiles):
            act(
                remote(
                    v.n, v.tn.at[t], v.tn_send.at[j - 1], v.tn_recv.at[t], me, (t + j) % tiles
                )
            )

    own_notes.wait()
    own_weights.wait()
    for j in range(1, owners):
        s = (me + j) % owners
        received(v.n.at[s], v.note_recv.at[0, s])
        received(v.w.at[s], v.note_recv.at[1, s])
    tile_notes(go)
    copies = [
        pltpu.make_async_copy(v.n, v.tn.at[t], v.local_sem.at[1]),
        pltpu.make_async_copy(v.n, v.ns, v.local_sem.at[2]),
        pltpu.make_async_copy(v.w, v.ws, v.local_sem.at[4]),
    ]
    for copy in copies:
        copy.start()
    for copy in copies:
        copy.wait()

    def settle():
        for j in range(1, tiles):
            tt = (t + j) % tiles
            received(v.tn.at[tt], v.tn_recv.at[tt])
        tile_scalars = pltpu.make_async_copy(v.tn, v.ts, v.local_sem.at[1])
        tile_scalars.start()
        tile_scalars.wait()
        load_bank.wait()

    step = 2 * across
    count = (deep + 1) * step

    def stage(n, body, lead=None):
        k, sign, xj = n // step, n % 2, n % step // 2
        hops = k - (xj + across - 1) // across
        zs = z + hops * (2 * sign - 1)
        s = zs * across + (x + xj) % across
        cond = jnp.logical_and(
            jnp.logical_and(n >= 0, n < count), jnp.logical_and(zs >= 0, zs < deep)
        )
        cond = jnp.logical_and(cond, jnp.logical_and(hops >= 0, hops + 1 - sign > 0))
        cond = jnp.logical_and(cond, hops < deep)
        if lead is True:
            cond = jnp.logical_and(cond, xj == 0)
        elif lead is False:
            cond = jnp.logical_and(cond, xj > 0)
        pl.when(cond)(lambda: body(s, zs, xj))

    def arrive(s, zs, xj):
        received(v.f.at[s, t], v.f_recv.at[s])

        @pl.when(xj == 0)
        def _():
            along(go, s, zs, v.f.at[s, t], None)
            side_frames(go, s, v.f.at[s, t])

        near_rows(go, s, v.f.at[s, t])

        @pl.when(xj == 0)
        def _():
            received(v.c.at[s], v.c_recv.at[s])
            along(go, s, zs, None, v.c.at[s])
            pack(s, zs, lambda f: v.c[s, f], lambda xo: places(s, xo))

        @pl.when(xj > 0)
        def _():
            received(v.cp.at[s], v.cp_recv.at[s])

    place = lax.broadcasted_iota(jnp.int32, (rows, 1), 0)
    item = place // columns
    column = place % columns

    def later(value):
        return jnp.where(column == 0, 0.0, pltpu.roll(value, 1, 0))

    def sooner(value):
        return jnp.where(column == columns - 1, 0.0, pltpu.roll(value, rows - 1, 0))

    def compute(s, zs, xj):
        pl.when(has_above)(lambda: received(v.f.at[s, t_above], v.ft_recv.at[s, t_above]))
        pl.when(has_below)(lambda: received(v.f.at[s, t_below], v.ft_recv.at[s, t_below]))
        e = v.ns[s, x, 0, 0]
        spots = places(s, x)
        blank = jnp.zeros((rows, channels), bf16)

        def gather(tt):
            return jnp.concatenate(picked(spots, lambda f: v.f[s, tt, f]), axis=0)

        window = [
            jnp.where(has_above, gather(t_above), blank),
            gather(t),
            jnp.where(has_below, gather(t_below), blank),
        ]
        upstream = v.cp[s].reshape(rows, channels).astype(f32)
        weight = jnp.zeros((rows, 1), f32)
        for c in range(cap):
            weight = jnp.where(item == c, v.ws[s, 0, c], weight)

        def column_term(db):
            total = jnp.dot(window[0], v.bank[e, db], preferred_element_type=f32)
            for da in (1, 2):
                total = total + jnp.dot(
                    window[da], v.bank[e, 3 * da + db], preferred_element_type=f32
                )
            return total

        pre = column_term(1) + later(column_term(0)) + sooner(column_term(2))
        pre = pre.astype(bf16).astype(f32)
        squash = jax.nn.sigmoid(pre)
        activated = pre * squash
        slope = squash * (1.0 + pre * (1.0 - squash))
        v.act[s] = (weight * activated).astype(bf16).reshape(cap, columns, channels)
        sums = jnp.sum((upstream * activated).reshape(cap, columns, channels), axis=1)
        sums = jnp.broadcast_to(jnp.sum(sums, axis=1, keepdims=True), (cap, 128))
        sums = jnp.concatenate([sums, jnp.zeros((8 - cap, 128), f32)], axis=0)
        v.gate[s] = sums

        @pl.when(s != me)
        def _():
            gates(go, s)

        @pl.when(s == me)
        def _():
            gated_ref[me] = sums

        grad = (upstream * weight * slope).astype(bf16)
        turned = jnp.transpose(grad.astype(f32)).astype(bf16)
        for k in range(tiles):
            v.go[s, k] = turned[k * share : (k + 1) * share]
        v.gi[s, t] = v.go[s, t]
        slices(go, s)
        for da in (0, 2, 1):
            parts = [
                lax.dot_general(
                    grad,
                    v.bank[e, 3 * da + db],
                    (((1,), (1,)), ((), ())),
                    preferred_element_type=f32,
                )
                for db in range(3)
            ]
            total = parts[1] + sooner(parts[0]) + later(parts[2])
            total = total.astype(bf16).reshape(cap, columns, channels)
            if da == 1:
                v.bk[s] = total
            else:
                v.eo[s, da // 2] = total
        pl.when(has_above)(lambda: edge_up(go, s))
        pl.when(has_below)(lambda: edge_down(go, s))

    def rims(s):
        pl.when(has_above)(lambda: received(v.above.at[s], v.above_recv.at[s]))
        pl.when(has_below)(lambda: received(v.below.at[s], v.below_recv.at[s]))

    def spread_out(value, spots, load, f):
        for c in range(cap):
            value = value + jnp.where(spots[c] == f, load(c).astype(f32), 0.0)
        return value

    def back_rows(s):
        mine = places(s, x)
        upper = [jnp.where(has_above, p, -1) for p in tile_places(t_above, s)]
        lower = [jnp.where(has_below, p, -1) for p in tile_places(t_below, s)]

        def row(f):
            value = jnp.zeros((columns, channels), f32)
            value = spread_out(value, mine, lambda c: v.bk[s, c], f)
            value = spread_out(value, upper, lambda c: v.above[s, c], f)
            return spread_out(value, lower, lambda c: v.below[s, c], f)

        return row

    def to_side(s, zs, xj):
        rims(s)
        row = back_rows(s)
        for f in range(frames):
            v.sbo[xj - 1, zs, f] = row(f).astype(bf16)
        side_terms(go, s, zs, xj)

    def to_far(s, zs, xj):
        rims(s)
        for j in range(1, across):
            received(v.sbi.at[j - 1, zs], v.sb_recv.at[j - 1, zs])
            received(v.sai.at[j - 1, zs], v.sa_recv.at[j - 1, zs])
        row = back_rows(s)
        spots = [places(s, x)] + [places(s, (x + across - j) % across) for j in range(1, across)]
        for f in range(frames):
            first = row(f)
            second = spread_out(
                jnp.zeros((columns, channels), f32), spots[0], lambda c: v.act[s, c], f
            )
            for j in range(1, across):
                first = first + v.sbi[j - 1, zs, f].astype(f32)
                second = spread_out(second, spots[j], lambda c: v.sai[j - 1, zs, c], f)
            v.total[0, f] = first
            v.total[1, f] = second

        @pl.when(zs == z)
        def _():
            for f in range(frames):
                v.base[0, f] = v.total[0, f] + v.c[me, f].astype(f32)
                v.base[1, f] = v.total[1, f] + v.f[me, t, f].astype(f32)

        @pl.when(zs != z)
        def _():
            v.fo[zs] = v.total[...].astype(bf16)
            far_terms(go, zs)

    lane = lax.broadcasted_iota(jnp.int32, (1, rows), 1) % columns

    def weigh(s, zs, xj):
        gather_passed(s)
        for j in range(1, tiles):
            tt = (t + j) % tiles
            received(v.gi.at[s, tt], v.g_recv.at[s, tt])
        for tt in range(tiles):
            e = v.ts[tt, s, x, 0, 0]
            spots = tile_places(tt, s)
            span = slice(tt * rows, (tt + 1) * rows)
            for da in range(3):
                source = tt + da - 1
                if 0 <= source < tiles:
                    parts = picked(spots, lambda f: v.f[s, source, f])
                    v.xw[da, span] = jnp.concatenate(parts, axis=0)
                else:
                    v.xw[da, span] = jnp.zeros((rows, channels), bf16)
            g = v.gi[s, tt].astype(f32)
            moved = [
                jnp.where(lane == columns - 1, 0.0, pltpu.roll(g, rows - 1, 1)).astype(bf16),
                v.gi[s, tt],
                jnp.where(lane == 0, 0.0, pltpu.roll(g, 1, 1)).astype(bf16),
            ]
            for db in range(3):
                for k in range(experts):
                    v.gt[db, k * share : (k + 1) * share, span] = jnp.where(
                        e == k, moved[db], jnp.zeros_like(moved[db])
                    )
        for da in range(3):
            for db in range(3):
                term = jnp.dot(v.gt[db], v.xw[da], preferred_element_type=f32)
                grad_ref[:, 3 * da + db] += term.reshape(experts, share, channels)

    @pl.loop(0, count + (count + 2 * step))
    def _(n):
        pl.when(n == step)(settle)
        stage(n - step, compute)
        stage(n - 2 * step, to_side, lead=False)
        stage(n - (count + step), lambda s, zs, xj: gather_far(s))
        stage(n - (4 * step + 2), to_far, lead=True)
        stage(n - (count + 2 * step), weigh)
        stage(n - count, lambda s, zs, xj: far_rows(go, s))
        pl.when(n > 1)(lambda: stage(n, arrive))

    for k in range(1, deep):
        zs = (z + k) % deep
        received(v.fi.at[zs], v.fi_recv.at[zs])
    for f in range(frames):
        first, second = v.base[0, f], v.base[1, f]
        for k in range(1, deep):
            zs = (z + k) % deep
            first = first + v.fi[zs, 0, f].astype(f32)
            second = second + v.fi[zs, 1, f].astype(f32)
        input_ref[f] = first.astype(bf16)
        result_ref[f] = second.astype(bf16)

    for j in range(1, owners):
        s = (me + j) % owners
        received(gated_ref.at[s], v.gate_recv.at[s])
        gates(drain, s)
    send_notes(drain)
    tile_notes(drain)

    def finish(s, zs, xj):
        @pl.when(xj == 0)
        def _():
            along(drain, s, zs, v.f.at[s, t], v.c.at[s])
            side_frames(drain, s, v.f.at[s, t])
            side_packed(drain, s, zs)
            pl.when(zs != z)(lambda: far_terms(drain, zs))

        pl.when(xj > 0)(lambda: side_terms(drain, s, zs, xj))
        near_rows(drain, s, v.f.at[s, t])
        far_rows(drain, s)
        pass_on(drain, s)
        slices(drain, s)
        pl.when(has_above)(lambda: edge_up(drain, s))
        pl.when(has_below)(lambda: edge_down(drain, s))

    @pl.loop(0, count)
    def _(n):
        stage(n, finish)


def layer(frames, cot, note, weight, kernels, owners, tiles):
    deep, across = grid_of(owners)
    cores = 1 if tiles % 2 else 2
    high = tiles // cores
    count, columns, channels = frames.shape
    experts, taps, _, outputs = kernels.shape
    share = outputs // tiles
    cap = CAP
    rows = cap * columns
    dma = pltpu.SemaphoreType.DMA
    vmem, hbm = pl.BlockSpec(memory_space=pltpu.VMEM), pl.BlockSpec(memory_space=pltpu.HBM)
    bf16, f32, i32 = jnp.bfloat16, jnp.float32, jnp.int32
    beside, mates, far = (max(value - 1, 1) for value in (across, cores, high))
    others, peers = max(owners - 1, 1), max(tiles - 1, 1)
    scratch = dict(
        f=pltpu.VMEM((owners, tiles, count, columns, channels), bf16),
        c=pltpu.VMEM((owners, count, columns, channels), bf16),
        cp=pltpu.VMEM((owners, cap, columns, channels), bf16),
        cpo=pltpu.VMEM((beside, deep, cap, columns, channels), bf16),
        n=pltpu.VMEM((owners, across, 1, 128), i32),
        w=pltpu.VMEM((owners, 1, 128), f32),
        tn=pltpu.VMEM((tiles, owners, across, 1, 128), i32),
        os=pltpu.SMEM((owners, 1, 128), i32),
        ns=pltpu.SMEM((owners, across, 1, 128), i32),
        ws=pltpu.SMEM((owners, 1, 128), f32),
        ts=pltpu.SMEM((tiles, owners, across, 1, 128), i32),
        bank=pltpu.VMEM(kernels.shape, bf16),
        act=pltpu.VMEM((owners, cap, columns, channels), bf16),
        bk=pltpu.VMEM((owners, cap, columns, channels), bf16),
        eo=pltpu.VMEM((owners, 2, cap, columns, channels), bf16),
        above=pltpu.VMEM((owners, cap, columns, channels), bf16),
        below=pltpu.VMEM((owners, cap, columns, channels), bf16),
        go=pltpu.VMEM((owners, tiles, share, rows), bf16),
        gi=pltpu.VMEM((owners, tiles, share, rows), bf16),
        gate=pltpu.VMEM((owners, 8, 128), f32),
        sbo=pltpu.VMEM((beside, deep, count, columns, channels), bf16),
        sbi=pltpu.VMEM((beside, deep, count, columns, channels), bf16),
        sai=pltpu.VMEM((beside, deep, cap, columns, channels), bf16),
        fo=pltpu.VMEM((deep, 2, count, columns, channels), bf16),
        fi=pltpu.VMEM((deep, 2, count, columns, channels), bf16),
        total=pltpu.VMEM((2, count, columns, channels), f32),
        base=pltpu.VMEM((2, count, columns, channels), f32),
        xw=pltpu.VMEM((3, tiles * rows, channels), bf16),
        gt=pltpu.VMEM((3, experts * share, tiles * rows), bf16),
        local_sem=dma((6,)),
        spare_sem=dma((1,)),
        note_send=dma((2, others)), note_recv=dma((2, owners)),
        tn_send=dma((peers,)), tn_recv=dma((tiles,)),
        f_up=dma((owners,)), f_down=dma((owners,)), f_side=dma((beside, owners)), f_recv=dma((owners,)),
        c_up=dma((owners,)), c_down=dma((owners,)), c_recv=dma((owners,)),
        cp_send=dma((beside, deep)), cp_recv=dma((owners,)),
        near_send=dma((2, owners)), far_send=dma((far, owners)),
        pass_send=dma((far, cores, mates, owners)), ft_recv=dma((owners, tiles)),
        above_send=dma((owners,)), above_recv=dma((owners,)),
        below_send=dma((owners,)), below_recv=dma((owners,)),
        g_send=dma((peers, owners)), g_recv=dma((owners, tiles)),
        gate_send=dma((owners,)), gate_recv=dma((owners,)),
        sb_send=dma((beside, deep)), sb_recv=dma((beside, deep)),
        sa_send=dma((beside, deep)), sa_recv=dma((beside, deep)),
        fo_send=dma((deep,)), fi_recv=dma((deep,)),
    )
    held = 2 * frames.size * 4 * 2 + experts * taps * share * channels * 4 + owners * 8 * 128 * 4
    for ref in scratch.values():
        if ref.memory_space == pltpu.VMEM:
            held += math.prod(ref.shape) * jnp.dtype(ref.dtype).itemsize
    return pl.pallas_call(
        functools.partial(layer_kernel, deep, across, high, cores, tuple(scratch)),
        out_shape=[
            jax.ShapeDtypeStruct(frames.shape, bf16),
            jax.ShapeDtypeStruct(frames.shape, bf16),
            jax.ShapeDtypeStruct((owners, 8, 128), f32),
            jax.ShapeDtypeStruct((experts, taps, share, channels), f32),
        ],
        in_specs=[hbm, hbm, vmem, vmem, hbm],
        out_specs=[vmem] * 4,
        scratch_shapes=list(scratch.values()),
        compiler_params=pltpu.CompilerParams(
            collective_id=0, has_side_effects=True, vmem_limit_bytes=held + (8 << 20)
        ),
        name="layer",
    )(*(pltpu.with_memory_space_constraint(v, pltpu.HBM) for v in (frames, cot)), note, weight,
      pltpu.with_memory_space_constraint(kernels, pltpu.HBM))


def shards(frames, kernels, experts, counts, gate_weights, cotangent):
    owners = lax.axis_size("dp")
    tiles = lax.axis_size("tile")
    local = kernels.shape[0]
    chosen = experts[:, 0]
    frame_count, slots = chosen.shape
    active = jnp.arange(slots)[None, :] < counts[:, 0][:, None]
    owner_of = chosen // local
    hit = (owner_of[:, :, None] == jnp.arange(owners)) & active[:, :, None]
    wanted = jnp.any(hit, axis=1)
    position = jnp.cumsum(wanted.astype(jnp.int32), axis=0) - 1
    slot_map = wanted.T[:, None, :] & (
        position.T[:, None, :] == jnp.arange(CAP)[None, :, None]
    )
    request = jnp.max(jnp.where(hit, (chosen % local)[:, :, None], 0), axis=(0, 1))
    tile_gate = jnp.sum(jnp.where(hit, gate_weights[:, 0][:, :, None], 0.0), axis=1)
    weight = jnp.sum(jnp.where(slot_map, tile_gate.T[:, None, :], 0.0), axis=2)
    place = jnp.sum(
        jnp.where(slot_map, jnp.arange(1, frame_count + 1)[None, None, :], 0), axis=2
    ) - 1
    note = jnp.concatenate([request[:, None], place], axis=1).astype(jnp.int32)
    note = jnp.pad(note[:, None, :], ((0, 0), (0, 0), (0, 128 - note.shape[1])))
    weight = jnp.pad(weight[:, None, :], ((0, 0), (0, 0), (0, 128 - CAP)))
    result, input_grad, gated, kernel_part = layer(
        frames[:, 0], cotangent[:, 0], note, weight, kernels, owners, tiles
    )
    kernel_part = jnp.swapaxes(kernel_part, 2, 3)
    gated = gated[:, :CAP, 0]
    selected = jnp.sum(jnp.where(slot_map, gated[:, :, None], 0.0), axis=1)
    gate_grad = jnp.sum(jnp.where(hit, selected.T[:, None, :], 0.0), axis=2)
    return (result[:, None], input_grad[:, None], gate_grad[:, None, :], kernel_part)


def solution(mesh):
    return jax.shard_map(
        shards,
        mesh=mesh,
        in_specs=(
            P("dp", "tile", None, None),
            P("dp", None, None, None),
            P("dp", "tile", None),
            P("dp", "tile"),
            P("dp", "tile", None),
            P("dp", "tile", None, None),
        ),
        out_specs=(
            P("dp", "tile", None, None),
            P("dp", "tile", None, None),
            P("dp", "tile", None),
            P("dp", None, None, "tile"),
        ),
        check_vma=False,
    )
```

```python
import functools
import math
from types import SimpleNamespace

import jax
import jax.numpy as jnp
from jax import lax
from jax.experimental import pallas as pl
from jax.experimental.pallas import tpu as pltpu
from jax.sharding import PartitionSpec as P

CAP = 2


def grid_of(owners):
    across = 1
    while across * across * 4 <= owners:
        across *= 2
    while owners % across:
        across -= 1
    return owners // across, across


def remote(src, dst, send, recv, dp, tile):
    return pltpu.make_async_remote_copy(
        src_ref=src,
        dst_ref=dst,
        send_sem=send,
        recv_sem=recv,
        device_id=(dp, tile),
        device_id_type=pl.DeviceIdType.MESH,
    )


def go(copy):
    copy.start()


def drain(copy):
    copy.wait_send()


def layer_kernel(
    deep, across, high, cores, names,
    frames_hbm, cot_hbm, note_ref, weight_ref, bank_hbm,
    result_ref, input_ref, gated_ref, grad_ref, *rest,
):
    v = SimpleNamespace(**dict(zip(names, rest)))
    me, t = lax.axis_index("dp"), lax.axis_index("tile")
    z, x = lax.div(me, across), lax.rem(me, across)
    y, core = lax.div(t, cores), lax.rem(t, cores)
    owners, tiles = deep * across, high * cores
    _, _, frames, columns, channels = v.f.shape
    experts, taps, share, _ = grad_ref.shape
    cap = CAP
    rows = cap * columns
    has_above, has_below = t > 0, t < tiles - 1
    t_above, t_below = lax.rem(t + tiles - 1, tiles), lax.rem(t + 1, tiles)
    bf16, f32 = jnp.bfloat16, jnp.float32

    load_bank = pltpu.make_async_copy(bank_hbm, v.bank, v.local_sem.at[0])
    own_rows = pltpu.make_async_copy(frames_hbm, v.f.at[me, t], v.local_sem.at[3])
    own_rows.start()
    own_cot = pltpu.make_async_copy(cot_hbm, v.c.at[me], v.local_sem.at[5])
    own_cot.start()
    load_bank.start()
    own_scalars = pltpu.make_async_copy(note_ref, v.os, v.local_sem.at[4])
    own_scalars.start()

    barrier = pltpu.get_barrier_semaphore()
    for j in range(1, owners):
        pl.semaphore_signal(
            barrier, device_id=(lax.rem(me + j, owners), t), device_id_type=pl.DeviceIdType.MESH
        )
    for j in range(1, tiles):
        pl.semaphore_signal(
            barrier, device_id=(me, lax.rem(t + j, tiles)), device_id_type=pl.DeviceIdType.MESH
        )
    pl.semaphore_wait(barrier, owners - 1 + tiles - 1)

    def along(act, s, zs, fr, co):
        up = jnp.logical_and(zs <= z, z < deep - 1)
        down = jnp.logical_and(zs >= z, z > 0)
        if fr is not None:
            pl.when(up)(
                lambda: act(
                    remote(fr, v.f.at[s, t], v.f_up.at[zs], v.f_recv.at[s], me + across, t)
                )
            )
            pl.when(down)(
                lambda: act(
                    remote(fr, v.f.at[s, t], v.f_down.at[zs], v.f_recv.at[s], me - across, t)
                )
            )
        if co is not None:
            pl.when(up)(
                lambda: act(remote(co, v.c.at[s], v.c_up.at[zs], v.c_recv.at[zs], me + across, t))
            )
            pl.when(down)(
                lambda: act(remote(co, v.c.at[s], v.c_down.at[zs], v.c_recv.at[zs], me - across, t))
            )

    def side_frames(act, s, zs, fr):
        for j in range(1, across):
            act(
                remote(
                    fr, v.f.at[s, t], v.f_side.at[j - 1, zs], v.f_recv.at[s],
                    z * across + lax.rem(x + j, across), t,
                )
            )

    def side_packed(act, s, zs):
        for j in range(1, across):
            act(
                remote(
                    v.cpo.at[j - 1, zs], v.cp.at[s], v.cp_send.at[j - 1, zs], v.cp_recv.at[s],
                    z * across + lax.rem(x + j, across), t,
                )
            )

    def near_rows(act, s, fr):
        pl.when(has_below)(
            lambda: act(
                remote(fr, v.f.at[s, t], v.near_send.at[0, s], v.ft_recv.at[s, t], me, t + 1)
            )
        )
        pl.when(has_above)(
            lambda: act(
                remote(fr, v.f.at[s, t], v.near_send.at[1, s], v.ft_recv.at[s, t], me, t - 1)
            )
        )

    def far_rows(act, s):
        for j in range(1, high):
            yy = lax.rem(y + j, high)
            beside = jnp.logical_or(
                jnp.logical_and(yy == y + 1, core == cores - 1),
                jnp.logical_and(yy == y - 1, core == 0),
            )
            pl.when(jnp.logical_not(beside))(
                lambda j=j, yy=yy: act(
                    remote(
                        v.f.at[s, t], v.f.at[s, t], v.far_send.at[j - 1, s], v.ft_recv.at[s, t],
                        me, yy * cores + core,
                    )
                )
            )

    def entering(body):
        for j in range(1, high):
            yy = lax.rem(y + j, high)
            for c in range(cores):
                across_low = jnp.logical_and(yy == y - 1, c == cores - 1)
                across_high = jnp.logical_and(yy == y + 1, c == 0)
                straight = jnp.logical_not(jnp.logical_or(across_low, across_high))
                enters = jnp.logical_or(
                    jnp.logical_and(across_low, core == 0),
                    jnp.logical_or(
                        jnp.logical_and(across_high, core == cores - 1),
                        jnp.logical_and(straight, core == c),
                    ),
                )
                body(j, c, yy * cores + c, enters, straight)

    def pass_on(act, s):
        def one(j, c, tt, enters, straight):
            @pl.when(enters)
            def _():
                for i in range(1, cores):
                    act(
                        remote(
                            v.f.at[s, tt], v.f.at[s, tt], v.pass_send.at[j - 1, c, i - 1, s],
                            v.ft_recv.at[s, tt], me, y * cores + lax.rem(core + i, cores),
                        )
                    )

        entering(one)

    def gather_far(s):
        def one(j, c, tt, enters, straight):
            pl.when(jnp.logical_and(enters, straight))(
                lambda: received(v.f.at[s, tt], v.ft_recv.at[s, tt])
            )

        entering(one)
        pass_on(go, s)

    def gather_passed(s):
        def one(j, c, tt, enters, straight):
            pl.when(jnp.logical_not(enters))(
                lambda: received(v.f.at[s, tt], v.ft_recv.at[s, tt])
            )

        entering(one)

    def edge_down(act, s):
        act(
            remote(
                v.eo.at[s, 1], v.above.at[s], v.above_send.at[s], v.above_recv.at[s], me, t + 1
            )
        )

    def edge_up(act, s):
        act(
            remote(
                v.eo.at[s, 0], v.below.at[s], v.below_send.at[s], v.below_recv.at[s], me, t - 1
            )
        )

    def slices(s):
        for j in range(1, tiles):
            tt = lax.rem(t + j, tiles)
            go(remote(v.go.at[s, tt], v.gi.at[s, t], v.g_send.at[s], v.g_recv.at[s], me, tt))

    def gates(s):
        go(remote(v.gate.at[s], gated_ref.at[me], v.gate_send.at[0], v.gate_recv.at[0], s, t))

    def side_act(act, s, zs, xj):
        act(
            remote(
                v.act.at[s], v.sai.at[xj - 1, zs],
                v.sa_send.at[xj - 1, zs], v.sa_recv.at[xj - 1, zs],
                z * across + lax.rem(s, across), t,
            )
        )

    def side_back(act, s, zs, xj):
        act(
            remote(
                v.sbo.at[xj - 1, zs], v.sbi.at[xj - 1, zs],
                v.sb_send.at[xj - 1, zs], v.sb_recv.at[xj - 1, zs],
                z * across + lax.rem(s, across), t,
            )
        )

    def far_terms(act, zs, part):
        act(
            remote(
                v.fo.at[zs, part], v.fi.at[z, part],
                v.fo_send.at[part, zs], v.fi_recv.at[part, z], zs * across + x, t,
            )
        )

    def sent(ref, sem):
        remote(ref, ref, sem, v.spare_sem.at[0], me, t).wait_send()

    def received(ref, sem):
        remote(ref, ref, v.spare_sem.at[0], sem, me, t).wait_recv()

    def send_notes():
        for j in range(1, owners):
            peer = lax.rem(me + j, owners)
            go(
                remote(
                    note_ref.at[pl.ds(lax.div(peer, across) * across, across)], v.n.at[me],
                    v.note_send.at[0], v.note_recv.at[0], peer, t,
                )
            )
            go(
                remote(
                    weight_ref.at[peer], v.w.at[me],
                    v.note_send.at[1], v.note_recv.at[1], peer, t,
                )
            )

    send_notes()
    own_notes = pltpu.make_async_copy(
        note_ref.at[pl.ds(z * across, across)], v.n.at[me], v.local_sem.at[1]
    )
    own_notes.start()
    own_weights = pltpu.make_async_copy(weight_ref.at[me], v.w.at[me], v.local_sem.at[2])
    own_weights.start()
    own_rows.wait()
    along(go, me, z, v.f.at[me, t], None)
    side_frames(go, me, z, v.f.at[me, t])
    near_rows(go, me, v.f.at[me, t])
    own_cot.wait()
    along(go, me, z, None, v.c.at[me])

    def places(s, xo):
        return [v.ns[s, xo, 0, 1 + c] for c in range(cap)]

    def tile_places(tt, s):
        return [v.ts[tt, s, x, 0, 1 + c] for c in range(cap)]

    def picked(spots, load):
        parts = []
        for c in range(cap):
            value = jnp.zeros((columns, channels), bf16)
            for f in range(frames):
                value = jnp.where(spots[c] == f, load(f), value)
            parts.append(value)
        return parts

    def pack(s, zs, load, spots_of):
        for j in range(1, across):
            parts = picked(spots_of(lax.rem(x + j, across)), load)
            for c in range(cap):
                v.cpo[j - 1, zs, c] = parts[c]
        side_packed(go, s, zs)
        parts = picked(spots_of(x), load)
        for c in range(cap):
            v.cp[s, c] = parts[c]

    own_scalars.wait()
    pack(
        me, z, lambda f: v.c[me, f],
        lambda xo: [v.os[z * across + xo, 0, 1 + c] for c in range(cap)],
    )

    @pl.when(jnp.logical_not(has_above))
    def _():
        v.above[...] = jnp.zeros_like(v.above)

    @pl.when(jnp.logical_not(has_below))
    def _():
        v.below[...] = jnp.zeros_like(v.below)

    @pl.loop(0, experts)
    def _(k):
        grad_ref[k] = jnp.zeros_like(grad_ref[k])

    def tile_notes():
        for j in range(1, tiles):
            go(remote(v.n, v.tn.at[t], v.tn_send.at[0], v.tn_recv.at[0], me, lax.rem(t + j, tiles)))

    own_notes.wait()
    own_weights.wait()
    received(v.n.at[pl.ds(0, owners - 1)], v.note_recv.at[0])
    received(v.w.at[pl.ds(0, owners - 1)], v.note_recv.at[1])
    tile_notes()
    copies = [
        pltpu.make_async_copy(v.n, v.tn.at[t], v.local_sem.at[1]),
        pltpu.make_async_copy(v.n, v.ns, v.local_sem.at[2]),
        pltpu.make_async_copy(v.w, v.ws, v.local_sem.at[4]),
    ]
    for copy in copies:
        copy.start()
    for copy in copies:
        copy.wait()

    def settle():
        received(v.tn.at[pl.ds(0, tiles - 1)], v.tn_recv.at[0])
        tile_scalars = pltpu.make_async_copy(v.tn, v.ts, v.local_sem.at[1])
        tile_scalars.start()
        tile_scalars.wait()

    step = 2 * across
    count = (deep + 1) * step

    def stage(n, body, lead=None):
        k, slot = lax.div(n, step), lax.rem(n, step)
        sign, xj = lax.rem(slot, 2), lax.div(slot, 2)
        hops = k - lax.div(xj + across - 1, across)
        zs = z + hops * (2 * sign - 1)
        s = zs * across + lax.rem(x + xj, across)
        cond = jnp.logical_and(
            jnp.logical_and(n >= 0, n < count), jnp.logical_and(zs >= 0, zs < deep)
        )
        cond = jnp.logical_and(cond, jnp.logical_and(hops >= 0, hops + 1 - sign > 0))
        cond = jnp.logical_and(cond, hops < deep)
        if lead is True:
            cond = jnp.logical_and(cond, jnp.logical_and(xj == 0, n > 0))
        elif lead is False:
            cond = jnp.logical_and(cond, xj > 0)
        pl.when(cond)(lambda: body(s, zs, xj))

    def arrive(s, zs, xj):
        received(v.f.at[s, t], v.f_recv.at[s])

        @pl.when(xj == 0)
        def _():
            along(go, s, zs, v.f.at[s, t], None)
            side_frames(go, s, zs, v.f.at[s, t])

        near_rows(go, s, v.f.at[s, t])

        @pl.when(xj == 0)
        def _():
            received(v.c.at[s], v.c_recv.at[zs])
            along(go, s, zs, None, v.c.at[s])
            pack(s, zs, lambda f: v.c[s, f], lambda xo: places(s, xo))

        @pl.when(xj > 0)
        def _():
            received(v.cp.at[s], v.cp_recv.at[s])

    place = lax.broadcasted_iota(jnp.int32, (rows, 1), 0)
    item = place // columns
    column = place % columns

    def later(value):
        return jnp.where(column == 0, 0.0, pltpu.roll(value, 1, 0))

    def sooner(value):
        return jnp.where(column == columns - 1, 0.0, pltpu.roll(value, rows - 1, 0))

    def compute(s, zs, xj):
        pl.when(has_above)(lambda: received(v.f.at[s, t_above], v.ft_recv.at[s, t_above]))
        pl.when(has_below)(lambda: received(v.f.at[s, t_below], v.ft_recv.at[s, t_below]))
        e = v.ns[s, x, 0, 0]
        spots = places(s, x)
        blank = jnp.zeros((rows, channels), bf16)

        def gather(tt):
            return jnp.concatenate(picked(spots, lambda f: v.f[s, tt, f]), axis=0)

        window = [
            jnp.where(has_above, gather(t_above), blank),
            gather(t),
            jnp.where(has_below, gather(t_below), blank),
        ]
        upstream = v.cp[s].reshape(rows, channels).astype(f32)
        weight = jnp.zeros((rows, 1), f32)
        for c in range(cap):
            weight = jnp.where(item == c, v.ws[s, 0, c], weight)

        def column_term(db):
            total = jnp.dot(window[0], v.bank[e, db], preferred_element_type=f32)
            for da in (1, 2):
                total = total + jnp.dot(
                    window[da], v.bank[e, 3 * da + db], preferred_element_type=f32
                )
            return total

        pre = column_term(1) + later(column_term(0)) + sooner(column_term(2))
        pre = pre.astype(bf16).astype(f32)
        squash = jax.nn.sigmoid(pre)
        activated = pre * squash
        slope = squash * (1.0 + pre * (1.0 - squash))
        v.act[s] = (weight * activated).astype(bf16).reshape(cap, columns, channels)
        pl.when(xj > 0)(lambda: side_act(go, s, zs, xj))
        sums = jnp.sum((upstream * activated).reshape(cap, columns, channels), axis=1)
        sums = jnp.broadcast_to(jnp.sum(sums, axis=1, keepdims=True), (cap, 128))
        sums = jnp.concatenate([sums, jnp.zeros((8 - cap, 128), f32)], axis=0)
        v.gate[s] = sums

        @pl.when(s != me)
        def _():
            gates(s)

        @pl.when(s == me)
        def _():
            gated_ref[me] = sums

        grad = (upstream * weight * slope).astype(bf16)
        turned = jnp.transpose(grad.astype(f32)).astype(bf16)
        for k in range(tiles):
            v.go[s, k] = turned[k * share : (k + 1) * share]
        v.gi[s, t] = v.go[s, t]
        slices(s)
        for da in (0, 2, 1):
            parts = [
                lax.dot_general(
                    grad,
                    v.bank[e, 3 * da + db],
                    (((1,), (1,)), ((), ())),
                    preferred_element_type=f32,
                )
                for db in range(3)
            ]
            total = parts[1] + sooner(parts[0]) + later(parts[2])
            total = total.astype(bf16).reshape(cap, columns, channels)
            if da == 1:
                v.bk[s] = total
            else:
                v.eo[s, da // 2] = total
        pl.when(has_above)(lambda: edge_up(go, s))
        pl.when(has_below)(lambda: edge_down(go, s))

    def rims(s):
        pl.when(has_above)(lambda: received(v.above.at[s], v.above_recv.at[s]))
        pl.when(has_below)(lambda: received(v.below.at[s], v.below_recv.at[s]))

    def spread_out(value, spots, load, f):
        found = jnp.zeros((columns, channels), bf16)
        for c in range(cap):
            found = jnp.where(spots[c] == f, load(c), found)
        return value + found.astype(f32)

    def back_rows(s):
        mine = places(s, x)
        upper = [jnp.where(has_above, p, -1) for p in tile_places(t_above, s)]
        lower = [jnp.where(has_below, p, -1) for p in tile_places(t_below, s)]

        def row(f):
            value = jnp.zeros((columns, channels), f32)
            value = spread_out(value, mine, lambda c: v.bk[s, c], f)
            value = spread_out(value, upper, lambda c: v.above[s, c], f)
            return spread_out(value, lower, lambda c: v.below[s, c], f)

        return row

    def to_side(s, zs, xj):
        rims(s)
        row = back_rows(s)
        for f in range(frames):
            v.sbo[xj - 1, zs, f] = row(f).astype(bf16)
        side_back(go, s, zs, xj)

    def far_act(s, zs, xj):
        for j in range(1, across):
            received(v.sai.at[j - 1, zs], v.sa_recv.at[j - 1, zs])
        spots = [places(s, x)] + [
            places(s, lax.rem(x + across - j, across)) for j in range(1, across)
        ]
        for f in range(frames):
            value = spread_out(
                jnp.zeros((columns, channels), f32), spots[0], lambda c: v.act[s, c], f
            )
            for j in range(1, across):
                value = spread_out(value, spots[j], lambda c: v.sai[j - 1, zs, c], f)
            v.total[1, f] = value

        @pl.when(zs == z)
        def _():
            for f in range(frames):
                v.base[1, f] = v.total[1, f] + v.f[me, t, f].astype(f32)

        @pl.when(zs != z)
        def _():
            v.fo[zs, 1] = v.total[1].astype(bf16)
            far_terms(go, zs, 1)

    def far_back(s, zs, xj):
        rims(s)
        for j in range(1, across):
            received(v.sbi.at[j - 1, zs], v.sb_recv.at[j - 1, zs])
        row = back_rows(s)
        for f in range(frames):
            value = row(f)
            for j in range(1, across):
                value = value + v.sbi[j - 1, zs, f].astype(f32)
            v.total[0, f] = value

        @pl.when(zs == z)
        def _():
            for f in range(frames):
                v.base[0, f] = v.total[0, f] + v.c[me, f].astype(f32)

        @pl.when(zs != z)
        def _():
            v.fo[zs, 0] = v.total[0].astype(bf16)
            far_terms(go, zs, 0)

    lane = lax.broadcasted_iota(jnp.int32, (1, rows), 1) % columns

    def weigh(s, zs, xj):
        gather_passed(s)
        received(v.gi.at[s, pl.ds(0, tiles - 1)], v.g_recv.at[s])
        for tt in range(tiles):
            e = v.ts[tt, s, x, 0, 0]
            spots = tile_places(tt, s)
            span = slice(tt * rows, (tt + 1) * rows)
            for da in range(3):
                source = tt + da - 1
                if 0 <= source < tiles:
                    parts = picked(spots, lambda f: v.f[s, source, f])
                    v.xw[da, span] = jnp.concatenate(parts, axis=0)
                else:
                    v.xw[da, span] = jnp.zeros((rows, channels), bf16)
            g = v.gi[s, tt].astype(f32)
            moved = [
                jnp.where(lane == columns - 1, 0.0, pltpu.roll(g, rows - 1, 1)).astype(bf16),
                v.gi[s, tt],
                jnp.where(lane == 0, 0.0, pltpu.roll(g, 1, 1)).astype(bf16),
            ]
            for db in range(3):
                for k in range(experts):
                    v.gt[db, k * share : (k + 1) * share, span] = jnp.where(
                        e == k, moved[db], jnp.zeros_like(moved[db])
                    )
        for da in range(3):
            for db in range(3):
                term = jnp.dot(v.gt[db], v.xw[da], preferred_element_type=f32)
                grad_ref[:, 3 * da + db] += term.reshape(experts, share, channels)

    @pl.loop(0, count + (4 * step + 2))
    def _(n):
        pl.when(n == step)(load_bank.wait)
        pl.when(n == (step + 3))(settle)
        stage(n - step, compute)
        stage(n - (step + 3), to_side, lead=False)
        stage(n - 4 * step, far_act, lead=True)
        stage(n - (4 * step + 2), far_back, lead=True)
        stage(n - (4 * step + 2), lambda s, zs, xj: far_rows(go, s))
        pl.when(n > 1)(lambda: stage(n, arrive))

    @pl.loop(0, count + 2)
    def _(n):
        stage(n, lambda s, zs, xj: gather_far(s))
        stage(n - 2, weigh)

    some = pl.ds(0, owners - 1)
    received(gated_ref.at[some], v.gate_recv.at[0])
    sent(v.gate.at[some], v.gate_send.at[0])
    sent(v.n.at[some], v.note_send.at[0])
    sent(v.w.at[some], v.note_send.at[1])
    sent(v.tn.at[pl.ds(0, tiles - 1)], v.tn_send.at[0])

    def finish(s, zs, xj):
        @pl.when(xj == 0)
        def _():
            along(drain, s, zs, v.f.at[s, t], v.c.at[s])
            side_frames(drain, s, zs, v.f.at[s, t])
            side_packed(drain, s, zs)
            for part in range(2):
                pl.when(zs != z)(lambda part=part: far_terms(drain, zs, part))

        @pl.when(xj > 0)
        def _():
            side_act(drain, s, zs, xj)
            side_back(drain, s, zs, xj)

        near_rows(drain, s, v.f.at[s, t])
        far_rows(drain, s)
        pass_on(drain, s)
        sent(v.go.at[s, pl.ds(0, tiles - 1)], v.g_send.at[s])
        pl.when(has_above)(lambda: edge_up(drain, s))
        pl.when(has_below)(lambda: edge_down(drain, s))

    @pl.loop(0, count)
    def _(n):
        stage(n, finish)

    far_act(me, z, 0)
    far_back(me, z, 0)
    for k in range(1, deep):
        zs = lax.rem(z + k, deep)
        for part in range(2):
            received(v.fi.at[zs, part], v.fi_recv.at[part, zs])
    for f in range(frames):
        first, second = v.base[0, f], v.base[1, f]
        for k in range(1, deep):
            zs = lax.rem(z + k, deep)
            first = first + v.fi[zs, 0, f].astype(f32)
            second = second + v.fi[zs, 1, f].astype(f32)
        input_ref[f] = first.astype(bf16)
        result_ref[f] = second.astype(bf16)


def layer(frames, cot, note, weight, kernels, owners, tiles):
    deep, across = grid_of(owners)
    cores = 1 if tiles % 2 else 2
    high = tiles // cores
    count, columns, channels = frames.shape
    experts, taps, _, outputs = kernels.shape
    share = outputs // tiles
    cap = CAP
    rows = cap * columns
    dma = pltpu.SemaphoreType.DMA
    vmem, hbm = pl.BlockSpec(memory_space=pltpu.VMEM), pl.BlockSpec(memory_space=pltpu.HBM)
    bf16, f32, i32 = jnp.bfloat16, jnp.float32, jnp.int32
    beside, mates, far = (max(value - 1, 1) for value in (across, cores, high))
    scratch = dict(
        f=pltpu.VMEM((owners, tiles, count, columns, channels), bf16),
        c=pltpu.VMEM((owners, count, columns, channels), bf16),
        cp=pltpu.VMEM((owners, cap, columns, channels), bf16),
        cpo=pltpu.VMEM((beside, deep, cap, columns, channels), bf16),
        n=pltpu.VMEM((owners, across, 1, 128), i32),
        w=pltpu.VMEM((owners, 1, 128), f32),
        tn=pltpu.VMEM((tiles, owners, across, 1, 128), i32),
        os=pltpu.SMEM((owners, 1, 128), i32),
        ns=pltpu.SMEM((owners, across, 1, 128), i32),
        ws=pltpu.SMEM((owners, 1, 128), f32),
        ts=pltpu.SMEM((tiles, owners, across, 1, 128), i32),
        bank=pltpu.VMEM(kernels.shape, bf16),
        act=pltpu.VMEM((owners, cap, columns, channels), bf16),
        bk=pltpu.VMEM((owners, cap, columns, channels), bf16),
        eo=pltpu.VMEM((owners, 2, cap, columns, channels), bf16),
        above=pltpu.VMEM((owners, cap, columns, channels), bf16),
        below=pltpu.VMEM((owners, cap, columns, channels), bf16),
        go=pltpu.VMEM((owners, tiles, share, rows), bf16),
        gi=pltpu.VMEM((owners, tiles, share, rows), bf16),
        gate=pltpu.VMEM((owners, 8, 128), f32),
        sbo=pltpu.VMEM((beside, deep, count, columns, channels), bf16),
        sbi=pltpu.VMEM((beside, deep, count, columns, channels), bf16),
        sai=pltpu.VMEM((beside, deep, cap, columns, channels), bf16),
        fo=pltpu.VMEM((deep, 2, count, columns, channels), bf16),
        fi=pltpu.VMEM((deep, 2, count, columns, channels), bf16),
        total=pltpu.VMEM((2, count, columns, channels), f32),
        base=pltpu.VMEM((2, count, columns, channels), f32),
        xw=pltpu.VMEM((3, tiles * rows, channels), bf16),
        gt=pltpu.VMEM((3, experts * share, tiles * rows), bf16),
        local_sem=dma((6,)),
        spare_sem=dma((1,)),
        note_send=dma((2,)), note_recv=dma((2,)),
        tn_send=dma((1,)), tn_recv=dma((1,)),
        f_up=dma((deep,)), f_down=dma((deep,)), f_side=dma((beside, deep)), f_recv=dma((owners,)),
        c_up=dma((deep,)), c_down=dma((deep,)), c_recv=dma((deep,)),
        cp_send=dma((beside, deep)), cp_recv=dma((owners,)),
        near_send=dma((2, owners)), far_send=dma((far, owners)),
        pass_send=dma((far, cores, mates, owners)), ft_recv=dma((owners, tiles)),
        above_send=dma((owners,)), above_recv=dma((owners,)),
        below_send=dma((owners,)), below_recv=dma((owners,)),
        g_send=dma((owners,)), g_recv=dma((owners,)),
        gate_send=dma((1,)), gate_recv=dma((1,)),
        sb_send=dma((beside, deep)), sb_recv=dma((beside, deep)),
        sa_send=dma((beside, deep)), sa_recv=dma((beside, deep)),
        fo_send=dma((2, deep)), fi_recv=dma((2, deep)),
    )
    held = 2 * frames.size * 4 * 2 + experts * taps * share * channels * 4 + owners * 8 * 128 * 4
    for ref in scratch.values():
        if ref.memory_space == pltpu.VMEM:
            held += math.prod(ref.shape) * jnp.dtype(ref.dtype).itemsize
    return pl.pallas_call(
        functools.partial(layer_kernel, deep, across, high, cores, tuple(scratch)),
        out_shape=[
            jax.ShapeDtypeStruct(frames.shape, bf16),
            jax.ShapeDtypeStruct(frames.shape, bf16),
            jax.ShapeDtypeStruct((owners, 8, 128), f32),
            jax.ShapeDtypeStruct((experts, taps, share, channels), f32),
        ],
        in_specs=[hbm, hbm, vmem, vmem, hbm],
        out_specs=[vmem] * 4,
        scratch_shapes=list(scratch.values()),
        compiler_params=pltpu.CompilerParams(
            collective_id=0, has_side_effects=True, vmem_limit_bytes=held + (8 << 20)
        ),
        name="layer",
    )(
        pltpu.with_memory_space_constraint(frames, pltpu.HBM),
        pltpu.with_memory_space_constraint(cot, pltpu.HBM),
        note,
        weight,
        pltpu.with_memory_space_constraint(kernels, pltpu.HBM),
    )


def settle_kernel(count, *refs):
    sems = refs[2 * count]
    copies = [
        pltpu.make_async_copy(refs[i], refs[count + i], sems.at[i]) for i in range(count)
    ]
    for copy in copies:
        copy.start()
    for copy in copies:
        copy.wait()


def settled(*arrays):
    count = len(arrays)
    anywhere = pl.BlockSpec(memory_space=pl.ANY)
    return pl.pallas_call(
        functools.partial(settle_kernel, count),
        out_shape=[jax.ShapeDtypeStruct(a.shape, a.dtype) for a in arrays],
        in_specs=[anywhere] * count,
        out_specs=[pl.BlockSpec(memory_space=pltpu.HBM)] * count,
        scratch_shapes=[pltpu.SemaphoreType.DMA((count,))],
        compiler_params=pltpu.CompilerParams(vmem_limit_bytes=1 << 20),
        name="settled",
    )(*arrays)


def shards(frames, kernels, experts, counts, gate_weights, cotangent):
    owners = lax.axis_size("dp")
    tiles = lax.axis_size("tile")
    local = kernels.shape[0]
    chosen = experts[:, 0]
    frame_count, slots = chosen.shape
    active = jnp.arange(slots)[None, :] < counts[:, 0][:, None]
    owner_of = chosen // local
    hit = (owner_of[:, :, None] == jnp.arange(owners)) & active[:, :, None]
    wanted = jnp.any(hit, axis=1)
    position = jnp.cumsum(wanted.astype(jnp.int32), axis=0) - 1
    slot_map = wanted.T[:, None, :] & (
        position.T[:, None, :] == jnp.arange(CAP)[None, :, None]
    )
    request = jnp.max(jnp.where(hit, (chosen % local)[:, :, None], 0), axis=(0, 1))
    tile_gate = jnp.sum(jnp.where(hit, gate_weights[:, 0][:, :, None], 0.0), axis=1)
    weight = jnp.sum(jnp.where(slot_map, tile_gate.T[:, None, :], 0.0), axis=2)
    place = jnp.sum(
        jnp.where(slot_map, jnp.arange(1, frame_count + 1)[None, None, :], 0), axis=2
    ) - 1
    note = jnp.concatenate([request[:, None], place], axis=1).astype(jnp.int32)
    note = jnp.pad(note[:, None, :], ((0, 0), (0, 0), (0, 128 - note.shape[1])))
    weight = jnp.pad(weight[:, None, :], ((0, 0), (0, 0), (0, 128 - CAP)))
    result, input_grad, gated, kernel_part = layer(
        frames[:, 0], cotangent[:, 0], note, weight, kernels, owners, tiles
    )
    result, input_grad, kernel_part = settled(result, input_grad, kernel_part)
    kernel_part = jnp.swapaxes(kernel_part, 2, 3)
    gated = gated[:, :CAP, 0]
    selected = jnp.sum(jnp.where(slot_map, gated[:, :, None], 0.0), axis=1)
    gate_grad = jnp.sum(jnp.where(hit, selected.T[:, None, :], 0.0), axis=2)
    return (result[:, None], input_grad[:, None], gate_grad[:, None, :], kernel_part)


def solution(mesh):
    return jax.shard_map(
        shards,
        mesh=mesh,
        in_specs=(
            P("dp", "tile", None, None),
            P("dp", None, None, None),
            P("dp", "tile", None),
            P("dp", "tile"),
            P("dp", "tile", None),
            P("dp", "tile", None, None),
        ),
        out_specs=(
            P("dp", "tile", None, None),
            P("dp", "tile", None, None),
            P("dp", "tile", None),
            P("dp", None, None, "tile"),
        ),
        check_vma=False,
    )
```

```python
import functools
import math
from types import SimpleNamespace

import jax
import jax.numpy as jnp
from jax import lax
from jax.experimental import pallas as pl
from jax.experimental.pallas import tpu as pltpu
from jax.sharding import PartitionSpec as P

CAP = 2


def grid_of(owners):
    across = 1
    while across * across * 4 <= owners:
        across *= 2
    while owners % across:
        across -= 1
    return owners // across, across


def remote(src, dst, send, recv, dp, tile):
    return pltpu.make_async_remote_copy(
        src_ref=src,
        dst_ref=dst,
        send_sem=send,
        recv_sem=recv,
        device_id=(dp, tile),
        device_id_type=pl.DeviceIdType.MESH,
    )


def go(copy):
    copy.start()


def drain(copy):
    copy.wait_send()


def layer_kernel(
    deep, across, high, cores, names,
    frames_hbm, cot_hbm, ids_hbm, counts_hbm, gates_hbm, bank_hbm,
    result_ref, input_ref, gate_ref, grad_ref, *rest,
):
    v = SimpleNamespace(**dict(zip(names, rest)))
    me, t = lax.axis_index("dp"), lax.axis_index("tile")
    z, x = lax.div(me, across), lax.rem(me, across)
    y, core = lax.div(t, cores), lax.rem(t, cores)
    owners, tiles = deep * across, high * cores
    _, _, frames, columns, channels = v.f.shape
    experts, taps, share, _ = grad_ref.shape
    cap = CAP
    rows = cap * columns
    has_above, has_below = t > 0, t < tiles - 1
    t_above, t_below = lax.rem(t + tiles - 1, tiles), lax.rem(t + 1, tiles)
    bf16, f32 = jnp.bfloat16, jnp.float32

    load_bank = pltpu.make_async_copy(bank_hbm, v.bank, v.local_sem.at[0])
    lists = [
        pltpu.make_async_copy(ids_hbm, v.ids, v.local_sem.at[1]),
        pltpu.make_async_copy(counts_hbm, v.counts, v.local_sem.at[2]),
        pltpu.make_async_copy(gates_hbm, v.gates, v.local_sem.at[4]),
    ]
    for copy in lists:
        copy.start()
    own_rows = pltpu.make_async_copy(frames_hbm, v.f.at[me, t], v.local_sem.at[3])
    own_rows.start()
    own_cot = pltpu.make_async_copy(cot_hbm, v.c.at[me], v.local_sem.at[5])
    own_cot.start()
    load_bank.start()

    barrier = pltpu.get_barrier_semaphore()
    for j in range(1, owners):
        pl.semaphore_signal(
            barrier, device_id=(lax.rem(me + j, owners), t), device_id_type=pl.DeviceIdType.MESH
        )
    for j in range(1, tiles):
        pl.semaphore_signal(
            barrier, device_id=(me, lax.rem(t + j, tiles)), device_id_type=pl.DeviceIdType.MESH
        )

    for copy in lists:
        copy.wait()
    slots = v.ids.shape[2]
    lanes = lax.broadcasted_iota(jnp.int32, (1, 128), 1)

    def owner_at(f, j):
        return jnp.where(j < v.counts[0, f], lax.div(v.ids[f, 0, j], experts), -1)

    wanted = jnp.zeros((1, 128), jnp.int32)
    listed = jnp.zeros((1, 128), jnp.int32)
    spot = [jnp.full((1, 128), -1, jnp.int32) for _ in range(cap)]
    share_of = [jnp.zeros((1, 128), f32) for _ in range(cap)]
    for f in range(frames):
        hit = jnp.zeros((1, 128), jnp.int32)
        gate = jnp.zeros((1, 128), f32)
        for j in range(slots):
            here = lanes == owner_at(f, j)
            hit = jnp.where(here, 1, hit)
            gate = jnp.where(here, v.gates[f, 0, j], gate)
            wanted = jnp.where(here, lax.rem(v.ids[f, 0, j], experts), wanted)
        for c in range(cap):
            taken = jnp.logical_and(hit == 1, listed == c)
            spot[c] = jnp.where(taken, f, spot[c])
            share_of[c] = jnp.where(taken, gate, share_of[c])
        listed = listed + hit
    asked = jnp.concatenate(
        [wanted] + spot + [jnp.zeros((127 - cap, 128), jnp.int32)], axis=0
    )
    shares = jnp.concatenate(share_of + [jnp.zeros((128 - cap, 128), f32)], axis=0)
    asked, shares = jnp.transpose(asked), jnp.transpose(shares)
    for o in range(owners):
        v.note[o] = asked[o : o + 1]
        v.weight[o] = shares[o : o + 1]
    own_scalars = pltpu.make_async_copy(v.note, v.os, v.local_sem.at[4])
    own_scalars.start()

    pl.semaphore_wait(barrier, owners - 1 + tiles - 1)

    def along(act, s, zs, fr, co):
        up = jnp.logical_and(zs <= z, z < deep - 1)
        down = jnp.logical_and(zs >= z, z > 0)
        if fr is not None:
            pl.when(up)(
                lambda: act(
                    remote(fr, v.f.at[s, t], v.f_up.at[zs], v.f_recv.at[s], me + across, t)
                )
            )
            pl.when(down)(
                lambda: act(
                    remote(fr, v.f.at[s, t], v.f_down.at[zs], v.f_recv.at[s], me - across, t)
                )
            )
        if co is not None:
            pl.when(up)(
                lambda: act(remote(co, v.c.at[s], v.c_up.at[zs], v.c_recv.at[zs], me + across, t))
            )
            pl.when(down)(
                lambda: act(remote(co, v.c.at[s], v.c_down.at[zs], v.c_recv.at[zs], me - across, t))
            )

    def side_frames(act, s, zs, fr):
        for j in range(1, across):
            act(
                remote(
                    fr, v.f.at[s, t], v.f_side.at[j - 1, zs], v.f_recv.at[s],
                    z * across + lax.rem(x + j, across), t,
                )
            )

    def side_packed(act, s, zs):
        for j in range(1, across):
            act(
                remote(
                    v.cpo.at[j - 1, zs], v.cp.at[s], v.cp_send.at[j - 1, zs], v.cp_recv.at[s],
                    z * across + lax.rem(x + j, across), t,
                )
            )

    def near_rows(act, s, fr):
        pl.when(has_below)(
            lambda: act(
                remote(fr, v.f.at[s, t], v.near_send.at[0, s], v.ft_recv.at[s, t], me, t + 1)
            )
        )
        pl.when(has_above)(
            lambda: act(
                remote(fr, v.f.at[s, t], v.near_send.at[1, s], v.ft_recv.at[s, t], me, t - 1)
            )
        )

    def far_rows(act, s):
        for j in range(1, high):
            yy = lax.rem(y + j, high)
            beside = jnp.logical_or(
                jnp.logical_and(yy == y + 1, core == cores - 1),
                jnp.logical_and(yy == y - 1, core == 0),
            )
            pl.when(jnp.logical_not(beside))(
                lambda j=j, yy=yy: act(
                    remote(
                        v.f.at[s, t], v.f.at[s, t], v.far_send.at[j - 1, s], v.ft_recv.at[s, t],
                        me, yy * cores + core,
                    )
                )
            )

    def entering(body):
        for j in range(1, high):
            yy = lax.rem(y + j, high)
            for c in range(cores):
                across_low = jnp.logical_and(yy == y - 1, c == cores - 1)
                across_high = jnp.logical_and(yy == y + 1, c == 0)
                straight = jnp.logical_not(jnp.logical_or(across_low, across_high))
                enters = jnp.logical_or(
                    jnp.logical_and(across_low, core == 0),
                    jnp.logical_or(
                        jnp.logical_and(across_high, core == cores - 1),
                        jnp.logical_and(straight, core == c),
                    ),
                )
                body(j, c, yy * cores + c, enters, straight)

    def pass_on(act, s):
        def one(j, c, tt, enters, straight):
            @pl.when(enters)
            def _():
                for i in range(1, cores):
                    act(
                        remote(
                            v.f.at[s, tt], v.f.at[s, tt], v.pass_send.at[j - 1, c, i - 1, s],
                            v.ft_recv.at[s, tt], me, y * cores + lax.rem(core + i, cores),
                        )
                    )

        entering(one)

    def gather_far(s):
        def one(j, c, tt, enters, straight):
            pl.when(jnp.logical_and(enters, straight))(
                lambda: received(v.f.at[s, tt], v.ft_recv.at[s, tt])
            )

        entering(one)
        pass_on(go, s)

    def gather_passed(s):
        def one(j, c, tt, enters, straight):
            pl.when(jnp.logical_not(enters))(
                lambda: received(v.f.at[s, tt], v.ft_recv.at[s, tt])
            )

        entering(one)

    def edge_down(act, s):
        act(
            remote(
                v.eo.at[s, 1], v.above.at[s], v.above_send.at[s], v.above_recv.at[s], me, t + 1
            )
        )

    def edge_up(act, s):
        act(
            remote(
                v.eo.at[s, 0], v.below.at[s], v.below_send.at[s], v.below_recv.at[s], me, t - 1
            )
        )

    def slices(s):
        for j in range(1, tiles):
            tt = lax.rem(t + j, tiles)
            go(remote(v.go.at[s, tt], v.gi.at[s, t], v.g_send.at[s], v.g_recv.at[s], me, tt))

    def gates(s):
        go(remote(v.gate.at[s], v.gated.at[me], v.gate_send.at[0], v.gate_recv.at[0], s, t))

    def side_act(act, s, zs, xj):
        act(
            remote(
                v.act.at[s], v.sai.at[xj - 1, zs],
                v.sa_send.at[xj - 1, zs], v.sa_recv.at[xj - 1, zs],
                z * across + lax.rem(s, across), t,
            )
        )

    def side_back(act, s, zs, xj):
        act(
            remote(
                v.sbo.at[xj - 1, zs], v.sbi.at[xj - 1, zs],
                v.sb_send.at[xj - 1, zs], v.sb_recv.at[xj - 1, zs],
                z * across + lax.rem(s, across), t,
            )
        )

    def far_terms(act, zs, part):
        act(
            remote(
                v.fo.at[zs, part], v.fi.at[z, part],
                v.fo_send.at[part, zs], v.fi_recv.at[part, z], zs * across + x, t,
            )
        )

    def sent(ref, sem):
        remote(ref, ref, sem, v.spare_sem.at[0], me, t).wait_send()

    def received(ref, sem):
        remote(ref, ref, v.spare_sem.at[0], sem, me, t).wait_recv()

    def send_notes():
        for j in range(1, owners):
            peer = lax.rem(me + j, owners)
            go(
                remote(
                    v.note.at[pl.ds(lax.div(peer, across) * across, across)], v.n.at[me],
                    v.note_send.at[0], v.note_recv.at[0], peer, t,
                )
            )
            go(
                remote(
                    v.weight.at[peer], v.w.at[me],
                    v.note_send.at[1], v.note_recv.at[1], peer, t,
                )
            )

    send_notes()
    own_notes = pltpu.make_async_copy(
        v.note.at[pl.ds(z * across, across)], v.n.at[me], v.local_sem.at[1]
    )
    own_notes.start()
    own_weights = pltpu.make_async_copy(v.weight.at[me], v.w.at[me], v.local_sem.at[2])
    own_weights.start()
    own_rows.wait()
    along(go, me, z, v.f.at[me, t], None)
    side_frames(go, me, z, v.f.at[me, t])
    near_rows(go, me, v.f.at[me, t])
    own_cot.wait()
    along(go, me, z, None, v.c.at[me])

    def places(s, xo):
        return [v.ns[s, xo, 0, 1 + c] for c in range(cap)]

    def tile_places(tt, s):
        return [v.ts[tt, s, x, 0, 1 + c] for c in range(cap)]

    def picked(spots, load):
        parts = []
        for c in range(cap):
            value = jnp.zeros((columns, channels), bf16)
            for f in range(frames):
                value = jnp.where(spots[c] == f, load(f), value)
            parts.append(value)
        return parts

    def pack(s, zs, load, spots_of):
        for j in range(1, across):
            parts = picked(spots_of(lax.rem(x + j, across)), load)
            for c in range(cap):
                v.cpo[j - 1, zs, c] = parts[c]
        side_packed(go, s, zs)
        parts = picked(spots_of(x), load)
        for c in range(cap):
            v.cp[s, c] = parts[c]

    own_scalars.wait()
    pack(
        me, z, lambda f: v.c[me, f],
        lambda xo: [v.os[z * across + xo, 0, 1 + c] for c in range(cap)],
    )

    @pl.when(jnp.logical_not(has_above))
    def _():
        v.above[...] = jnp.zeros_like(v.above)

    @pl.when(jnp.logical_not(has_below))
    def _():
        v.below[...] = jnp.zeros_like(v.below)

    @pl.loop(0, experts)
    def _(k):
        grad_ref[k] = jnp.zeros_like(grad_ref[k])

    def tile_notes():
        for j in range(1, tiles):
            go(remote(v.n, v.tn.at[t], v.tn_send.at[0], v.tn_recv.at[0], me, lax.rem(t + j, tiles)))

    own_notes.wait()
    own_weights.wait()
    received(v.n.at[pl.ds(0, owners - 1)], v.note_recv.at[0])
    received(v.w.at[pl.ds(0, owners - 1)], v.note_recv.at[1])
    tile_notes()
    copies = [
        pltpu.make_async_copy(v.n, v.tn.at[t], v.local_sem.at[1]),
        pltpu.make_async_copy(v.n, v.ns, v.local_sem.at[2]),
        pltpu.make_async_copy(v.w, v.ws, v.local_sem.at[4]),
    ]
    for copy in copies:
        copy.start()
    for copy in copies:
        copy.wait()

    def settle():
        received(v.tn.at[pl.ds(0, tiles - 1)], v.tn_recv.at[0])
        tile_scalars = pltpu.make_async_copy(v.tn, v.ts, v.local_sem.at[1])
        tile_scalars.start()
        tile_scalars.wait()

    step = 2 * across
    count = (deep + 1) * step

    def stage(n, body, lead=None):
        k, slot = lax.div(n, step), lax.rem(n, step)
        sign, xj = lax.rem(slot, 2), lax.div(slot, 2)
        hops = k - lax.div(xj + across - 1, across)
        zs = z + hops * (2 * sign - 1)
        s = zs * across + lax.rem(x + xj, across)
        cond = jnp.logical_and(
            jnp.logical_and(n >= 0, n < count), jnp.logical_and(zs >= 0, zs < deep)
        )
        cond = jnp.logical_and(cond, jnp.logical_and(hops >= 0, hops + 1 - sign > 0))
        cond = jnp.logical_and(cond, hops < deep)
        if lead is True:
            cond = jnp.logical_and(cond, jnp.logical_and(xj == 0, n > 0))
        elif lead is False:
            cond = jnp.logical_and(cond, xj > 0)
        pl.when(cond)(lambda: body(s, zs, xj))

    def arrive(s, zs, xj):
        received(v.f.at[s, t], v.f_recv.at[s])

        @pl.when(xj == 0)
        def _():
            along(go, s, zs, v.f.at[s, t], None)
            side_frames(go, s, zs, v.f.at[s, t])

        near_rows(go, s, v.f.at[s, t])

        @pl.when(xj == 0)
        def _():
            received(v.c.at[s], v.c_recv.at[zs])
            along(go, s, zs, None, v.c.at[s])
            pack(s, zs, lambda f: v.c[s, f], lambda xo: places(s, xo))

        @pl.when(xj > 0)
        def _():
            received(v.cp.at[s], v.cp_recv.at[s])

    place = lax.broadcasted_iota(jnp.int32, (rows, 1), 0)
    item = place // columns
    column = place % columns

    def later(value):
        return jnp.where(column == 0, 0.0, pltpu.roll(value, 1, 0))

    def sooner(value):
        return jnp.where(column == columns - 1, 0.0, pltpu.roll(value, rows - 1, 0))

    def compute(s, zs, xj):
        pl.when(has_above)(lambda: received(v.f.at[s, t_above], v.ft_recv.at[s, t_above]))
        pl.when(has_below)(lambda: received(v.f.at[s, t_below], v.ft_recv.at[s, t_below]))
        e = v.ns[s, x, 0, 0]
        spots = places(s, x)
        blank = jnp.zeros((rows, channels), bf16)

        def gather(tt):
            return jnp.concatenate(picked(spots, lambda f: v.f[s, tt, f]), axis=0)

        window = [
            jnp.where(has_above, gather(t_above), blank),
            gather(t),
            jnp.where(has_below, gather(t_below), blank),
        ]
        upstream = v.cp[s].reshape(rows, channels).astype(f32)
        weight = jnp.zeros((rows, 1), f32)
        for c in range(cap):
            weight = jnp.where(item == c, v.ws[s, 0, c], weight)

        def column_term(db):
            total = jnp.dot(window[0], v.bank[e, db], preferred_element_type=f32)
            for da in (1, 2):
                total = total + jnp.dot(
                    window[da], v.bank[e, 3 * da + db], preferred_element_type=f32
                )
            return total

        pre = column_term(1) + later(column_term(0)) + sooner(column_term(2))
        pre = pre.astype(bf16).astype(f32)
        squash = jax.nn.sigmoid(pre)
        activated = pre * squash
        slope = squash * (1.0 + pre * (1.0 - squash))
        v.act[s] = (weight * activated).astype(bf16).reshape(cap, columns, channels)
        pl.when(xj > 0)(lambda: side_act(go, s, zs, xj))
        sums = jnp.sum((upstream * activated).reshape(cap, columns, channels), axis=1)
        sums = jnp.broadcast_to(jnp.sum(sums, axis=1, keepdims=True), (cap, 128))
        sums = jnp.concatenate([sums, jnp.zeros((8 - cap, 128), f32)], axis=0)
        v.gate[s] = sums

        @pl.when(s != me)
        def _():
            gates(s)

        @pl.when(s == me)
        def _():
            v.gated[me] = sums

        grad = (upstream * weight * slope).astype(bf16)
        turned = jnp.transpose(grad.astype(f32)).astype(bf16)
        for k in range(tiles):
            v.go[s, k] = turned[k * share : (k + 1) * share]
        v.gi[s, t] = v.go[s, t]
        slices(s)
        for da in (0, 2, 1):
            parts = [
                lax.dot_general(
                    grad,
                    v.bank[e, 3 * da + db],
                    (((1,), (1,)), ((), ())),
                    preferred_element_type=f32,
                )
                for db in range(3)
            ]
            total = parts[1] + sooner(parts[0]) + later(parts[2])
            total = total.astype(bf16).reshape(cap, columns, channels)
            if da == 1:
                v.bk[s] = total
            else:
                v.eo[s, da // 2] = total
        pl.when(has_above)(lambda: edge_up(go, s))
        pl.when(has_below)(lambda: edge_down(go, s))

    def rims(s):
        pl.when(has_above)(lambda: received(v.above.at[s], v.above_recv.at[s]))
        pl.when(has_below)(lambda: received(v.below.at[s], v.below_recv.at[s]))

    def spread_out(value, spots, load, f):
        found = jnp.zeros((columns, channels), bf16)
        for c in range(cap):
            found = jnp.where(spots[c] == f, load(c), found)
        return value + found.astype(f32)

    def back_rows(s):
        mine = places(s, x)
        upper = [jnp.where(has_above, p, -1) for p in tile_places(t_above, s)]
        lower = [jnp.where(has_below, p, -1) for p in tile_places(t_below, s)]

        def row(f):
            value = jnp.zeros((columns, channels), f32)
            value = spread_out(value, mine, lambda c: v.bk[s, c], f)
            value = spread_out(value, upper, lambda c: v.above[s, c], f)
            return spread_out(value, lower, lambda c: v.below[s, c], f)

        return row

    def to_side(s, zs, xj):
        rims(s)
        row = back_rows(s)
        for f in range(frames):
            v.sbo[xj - 1, zs, f] = row(f).astype(bf16)
        side_back(go, s, zs, xj)

    def far_act(s, zs, xj):
        for j in range(1, across):
            received(v.sai.at[j - 1, zs], v.sa_recv.at[j - 1, zs])
        spots = [places(s, x)] + [
            places(s, lax.rem(x + across - j, across)) for j in range(1, across)
        ]
        for f in range(frames):
            value = spread_out(
                jnp.zeros((columns, channels), f32), spots[0], lambda c: v.act[s, c], f
            )
            for j in range(1, across):
                value = spread_out(value, spots[j], lambda c: v.sai[j - 1, zs, c], f)
            v.total[1, f] = value

        @pl.when(zs == z)
        def _():
            for f in range(frames):
                v.base[1, f] = v.total[1, f] + v.f[me, t, f].astype(f32)

        @pl.when(zs != z)
        def _():
            v.fo[zs, 1] = v.total[1].astype(bf16)
            far_terms(go, zs, 1)

    def far_back(s, zs, xj):
        rims(s)
        for j in range(1, across):
            received(v.sbi.at[j - 1, zs], v.sb_recv.at[j - 1, zs])
        row = back_rows(s)
        for f in range(frames):
            value = row(f)
            for j in range(1, across):
                value = value + v.sbi[j - 1, zs, f].astype(f32)
            v.total[0, f] = value

        @pl.when(zs == z)
        def _():
            for f in range(frames):
                v.base[0, f] = v.total[0, f] + v.c[me, f].astype(f32)

        @pl.when(zs != z)
        def _():
            v.fo[zs, 0] = v.total[0].astype(bf16)
            far_terms(go, zs, 0)

    lane = lax.broadcasted_iota(jnp.int32, (1, rows), 1) % columns

    def weigh(s, zs, xj):
        gather_passed(s)
        received(v.gi.at[s, pl.ds(0, tiles - 1)], v.g_recv.at[s])
        for tt in range(tiles):
            e = v.ts[tt, s, x, 0, 0]
            spots = tile_places(tt, s)
            span = slice(tt * rows, (tt + 1) * rows)
            for da in range(3):
                source = tt + da - 1
                if 0 <= source < tiles:
                    parts = picked(spots, lambda f: v.f[s, source, f])
                    v.xw[da, span] = jnp.concatenate(parts, axis=0)
                else:
                    v.xw[da, span] = jnp.zeros((rows, channels), bf16)
            g = v.gi[s, tt].astype(f32)
            moved = [
                jnp.where(lane == columns - 1, 0.0, pltpu.roll(g, rows - 1, 1)).astype(bf16),
                v.gi[s, tt],
                jnp.where(lane == 0, 0.0, pltpu.roll(g, 1, 1)).astype(bf16),
            ]
            for db in range(3):
                for k in range(experts):
                    first = (db * experts + k) * share
                    v.gt[first : first + share, span] = jnp.where(
                        e == k, moved[db], jnp.zeros_like(moved[db])
                    )
        for da in range(3):
            term = jnp.dot(v.gt[...], v.xw[da], preferred_element_type=f32)
            term = term.reshape(3, experts, share, channels)
            for db in range(3):
                grad_ref[:, 3 * da + db] += term[db]

    @pl.loop(0, count + (4 * step + 2))
    def _(n):
        pl.when(n == step)(load_bank.wait)
        pl.when(n == (step + 3))(settle)
        stage(n - step, compute)
        stage(n - (step + 3), to_side, lead=False)
        stage(n - 4 * step, far_act, lead=True)
        stage(n - (4 * step + 2), far_back, lead=True)
        stage(n - (4 * step + 2), lambda s, zs, xj: far_rows(go, s))
        pl.when(n > 1)(lambda: stage(n, arrive))

    @pl.loop(0, count + 2)
    def _(n):
        stage(n, lambda s, zs, xj: gather_far(s))
        stage(n - 2, weigh)

    some = pl.ds(0, owners - 1)
    received(v.gated.at[some], v.gate_recv.at[0])
    sent(v.gate.at[some], v.gate_send.at[0])
    for f in range(frames):
        at = jnp.full((1, 128), -1, jnp.int32)
        for j in range(slots):
            at = jnp.where(lanes == j, owner_at(f, j), at)
        found = jnp.zeros((1, 128), f32)
        for o in range(owners):
            for c in range(cap):
                owner = jnp.where(v.os[o, 0, 1 + c] == f, o, -2)
                found = jnp.where(at == owner, v.gated[o, c : c + 1], found)
        gate_ref[f] = found[:, :slots]
    sent(v.n.at[some], v.note_send.at[0])
    sent(v.w.at[some], v.note_send.at[1])
    sent(v.tn.at[pl.ds(0, tiles - 1)], v.tn_send.at[0])

    def finish(s, zs, xj):
        @pl.when(xj == 0)
        def _():
            along(drain, s, zs, v.f.at[s, t], v.c.at[s])
            side_frames(drain, s, zs, v.f.at[s, t])
            side_packed(drain, s, zs)
            for part in range(2):
                pl.when(zs != z)(lambda part=part: far_terms(drain, zs, part))

        @pl.when(xj > 0)
        def _():
            side_act(drain, s, zs, xj)
            side_back(drain, s, zs, xj)

        near_rows(drain, s, v.f.at[s, t])
        far_rows(drain, s)
        pass_on(drain, s)
        sent(v.go.at[s, pl.ds(0, tiles - 1)], v.g_send.at[s])
        pl.when(has_above)(lambda: edge_up(drain, s))
        pl.when(has_below)(lambda: edge_down(drain, s))

    @pl.loop(0, count)
    def _(n):
        stage(n, finish)

    far_act(me, z, 0)
    far_back(me, z, 0)
    for k in range(1, deep):
        zs = lax.rem(z + k, deep)
        for part in range(2):
            received(v.fi.at[zs, part], v.fi_recv.at[part, zs])
    for f in range(frames):
        first, second = v.base[0, f], v.base[1, f]
        for k in range(1, deep):
            zs = lax.rem(z + k, deep)
            first = first + v.fi[zs, 0, f].astype(f32)
            second = second + v.fi[zs, 1, f].astype(f32)
        input_ref[f] = first.astype(bf16)
        result_ref[f] = second.astype(bf16)


def layer(frames, cot, ids, counts, gates, kernels, owners, tiles):
    deep, across = grid_of(owners)
    cores = 1 if tiles % 2 else 2
    high = tiles // cores
    count, columns, channels = frames.shape
    experts, taps, _, outputs = kernels.shape
    share = outputs // tiles
    cap = CAP
    rows = cap * columns
    dma = pltpu.SemaphoreType.DMA
    vmem, hbm = pl.BlockSpec(memory_space=pltpu.VMEM), pl.BlockSpec(memory_space=pltpu.HBM)
    bf16, f32, i32 = jnp.bfloat16, jnp.float32, jnp.int32
    beside, mates, far = (max(value - 1, 1) for value in (across, cores, high))
    scratch = dict(
        f=pltpu.VMEM((owners, tiles, count, columns, channels), bf16),
        c=pltpu.VMEM((owners, count, columns, channels), bf16),
        cp=pltpu.VMEM((owners, cap, columns, channels), bf16),
        cpo=pltpu.VMEM((beside, deep, cap, columns, channels), bf16),
        n=pltpu.VMEM((owners, across, 1, 128), i32),
        w=pltpu.VMEM((owners, 1, 128), f32),
        tn=pltpu.VMEM((tiles, owners, across, 1, 128), i32),
        os=pltpu.SMEM((owners, 1, 128), i32),
        ns=pltpu.SMEM((owners, across, 1, 128), i32),
        ws=pltpu.SMEM((owners, 1, 128), f32),
        ts=pltpu.SMEM((tiles, owners, across, 1, 128), i32),
        bank=pltpu.VMEM(kernels.shape, bf16),
        act=pltpu.VMEM((owners, cap, columns, channels), bf16),
        bk=pltpu.VMEM((owners, cap, columns, channels), bf16),
        eo=pltpu.VMEM((owners, 2, cap, columns, channels), bf16),
        above=pltpu.VMEM((owners, cap, columns, channels), bf16),
        below=pltpu.VMEM((owners, cap, columns, channels), bf16),
        go=pltpu.VMEM((owners, tiles, share, rows), bf16),
        gi=pltpu.VMEM((owners, tiles, share, rows), bf16),
        gate=pltpu.VMEM((owners, 8, 128), f32),
        gated=pltpu.VMEM((owners, 8, 128), f32),
        ids=pltpu.SMEM(ids.shape, i32),
        counts=pltpu.SMEM(counts.shape, i32),
        gates=pltpu.SMEM(gates.shape, f32),
        note=pltpu.VMEM((owners, 1, 128), i32),
        weight=pltpu.VMEM((owners, 1, 128), f32),
        sbo=pltpu.VMEM((beside, deep, count, columns, channels), bf16),
        sbi=pltpu.VMEM((beside, deep, count, columns, channels), bf16),
        sai=pltpu.VMEM((beside, deep, cap, columns, channels), bf16),
        fo=pltpu.VMEM((deep, 2, count, columns, channels), bf16),
        fi=pltpu.VMEM((deep, 2, count, columns, channels), bf16),
        total=pltpu.VMEM((2, count, columns, channels), f32),
        base=pltpu.VMEM((2, count, columns, channels), f32),
        xw=pltpu.VMEM((3, tiles * rows, channels), bf16),
        gt=pltpu.VMEM((3 * experts * share, tiles * rows), bf16),
        local_sem=dma((6,)),
        spare_sem=dma((1,)),
        note_send=dma((2,)), note_recv=dma((2,)),
        tn_send=dma((1,)), tn_recv=dma((1,)),
        f_up=dma((deep,)), f_down=dma((deep,)), f_side=dma((beside, deep)), f_recv=dma((owners,)),
        c_up=dma((deep,)), c_down=dma((deep,)), c_recv=dma((deep,)),
        cp_send=dma((beside, deep)), cp_recv=dma((owners,)),
        near_send=dma((2, owners)), far_send=dma((far, owners)),
        pass_send=dma((far, cores, mates, owners)), ft_recv=dma((owners, tiles)),
        above_send=dma((owners,)), above_recv=dma((owners,)),
        below_send=dma((owners,)), below_recv=dma((owners,)),
        g_send=dma((owners,)), g_recv=dma((owners,)),
        gate_send=dma((1,)), gate_recv=dma((1,)),
        sb_send=dma((beside, deep)), sb_recv=dma((beside, deep)),
        sa_send=dma((beside, deep)), sa_recv=dma((beside, deep)),
        fo_send=dma((2, deep)), fi_recv=dma((2, deep)),
    )
    held = 2 * frames.size * 4 * 2 + experts * taps * share * channels * 4 + owners * 8 * 128 * 4
    for ref in scratch.values():
        if ref.memory_space == pltpu.VMEM:
            held += math.prod(ref.shape) * jnp.dtype(ref.dtype).itemsize
    return pl.pallas_call(
        functools.partial(layer_kernel, deep, across, high, cores, tuple(scratch)),
        out_shape=[
            jax.ShapeDtypeStruct(frames.shape, bf16),
            jax.ShapeDtypeStruct(frames.shape, bf16),
            jax.ShapeDtypeStruct(gates.shape, f32),
            jax.ShapeDtypeStruct((experts, taps, share, channels), f32),
        ],
        in_specs=[hbm] * 6,
        out_specs=[vmem] * 4,
        scratch_shapes=list(scratch.values()),
        compiler_params=pltpu.CompilerParams(
            collective_id=0, has_side_effects=True, vmem_limit_bytes=held + (8 << 20)
        ),
        name="layer",
    )(
        *(
            pltpu.with_memory_space_constraint(value, pltpu.HBM)
            for value in (frames, cot, ids, counts, gates, kernels)
        )
    )


def settle_kernel(count, *refs):
    sems = refs[2 * count]
    copies = [
        pltpu.make_async_copy(refs[i], refs[count + i], sems.at[i]) for i in range(count)
    ]
    for copy in copies:
        copy.start()
    for copy in copies:
        copy.wait()


def settled(*arrays):
    count = len(arrays)
    anywhere = pl.BlockSpec(memory_space=pl.ANY)
    return pl.pallas_call(
        functools.partial(settle_kernel, count),
        out_shape=[jax.ShapeDtypeStruct(a.shape, a.dtype) for a in arrays],
        in_specs=[anywhere] * count,
        out_specs=[pl.BlockSpec(memory_space=pltpu.HBM)] * count,
        scratch_shapes=[pltpu.SemaphoreType.DMA((count,))],
        compiler_params=pltpu.CompilerParams(vmem_limit_bytes=1 << 20),
        name="settled",
    )(*arrays)


def shards(frames, kernels, experts, counts, gate_weights, cotangent):
    owners = lax.axis_size("dp")
    tiles = lax.axis_size("tile")
    result, input_grad, gate_grad, kernel_part = settled(
        *layer(
            frames[:, 0], cotangent[:, 0], experts, counts.T, gate_weights, kernels, owners, tiles
        )
    )
    kernel_part = jnp.swapaxes(kernel_part, 2, 3)
    return (result[:, None], input_grad[:, None], gate_grad, kernel_part)


def solution(mesh):
    return jax.shard_map(
        shards,
        mesh=mesh,
        in_specs=(
            P("dp", "tile", None, None),
            P("dp", None, None, None),
            P("dp", "tile", None),
            P("dp", "tile"),
            P("dp", "tile", None),
            P("dp", "tile", None, None),
        ),
        out_specs=(
            P("dp", "tile", None, None),
            P("dp", "tile", None, None),
            P("dp", "tile", None),
            P("dp", None, None, "tile"),
        ),
        check_vma=False,
    )
```

```python
import functools
import math
from types import SimpleNamespace

import jax
import jax.numpy as jnp
from jax import lax
from jax.experimental import pallas as pl
from jax.experimental.pallas import tpu as pltpu
from jax.sharding import PartitionSpec as P

CAP = 2


def grid_of(owners):
    across = 1
    while across * across * 4 <= owners:
        across *= 2
    while owners % across:
        across -= 1
    return owners // across, across


def remote(src, dst, send, recv, dp, tile):
    return pltpu.make_async_remote_copy(
        src_ref=src,
        dst_ref=dst,
        send_sem=send,
        recv_sem=recv,
        device_id=(dp, tile),
        device_id_type=pl.DeviceIdType.MESH,
    )


def go(copy):
    copy.start()


def drain(copy):
    copy.wait_send()


def layer_kernel(
    deep, across, high, cores, names,
    frames_hbm, cot_hbm, ids_hbm, counts_hbm, gates_hbm, bank_hbm,
    result_ref, input_ref, gate_ref, grad_ref, *rest,
):
    v = SimpleNamespace(**dict(zip(names, rest)))
    me, t = lax.axis_index("dp"), lax.axis_index("tile")
    z, x = lax.div(me, across), lax.rem(me, across)
    y, core = lax.div(t, cores), lax.rem(t, cores)
    owners, tiles = deep * across, high * cores
    _, _, frames, columns, channels = v.f.shape
    experts, taps, share, _ = grad_ref.shape
    cap = CAP
    rows = cap * columns
    has_above, has_below = t > 0, t < tiles - 1
    t_above, t_below = lax.rem(t + tiles - 1, tiles), lax.rem(t + 1, tiles)
    bf16, f32 = jnp.bfloat16, jnp.float32

    load_bank = pltpu.make_async_copy(bank_hbm, v.bank, v.local_sem.at[0])
    lists = [
        pltpu.make_async_copy(ids_hbm, v.ids, v.local_sem.at[1]),
        pltpu.make_async_copy(counts_hbm, v.counts, v.local_sem.at[2]),
        pltpu.make_async_copy(gates_hbm, v.gates, v.local_sem.at[4]),
    ]
    for copy in lists:
        copy.start()
    own_rows = pltpu.make_async_copy(frames_hbm, v.f.at[me, t], v.local_sem.at[3])
    own_rows.start()
    own_cot = pltpu.make_async_copy(cot_hbm, v.c.at[me], v.local_sem.at[5])
    own_cot.start()
    load_bank.start()

    barrier = pltpu.get_barrier_semaphore()
    for j in range(1, owners):
        pl.semaphore_signal(
            barrier, device_id=(lax.rem(me + j, owners), t), device_id_type=pl.DeviceIdType.MESH
        )
    for j in range(1, tiles):
        pl.semaphore_signal(
            barrier, device_id=(me, lax.rem(t + j, tiles)), device_id_type=pl.DeviceIdType.MESH
        )

    for copy in lists:
        copy.wait()
    slots = v.ids.shape[2]
    lanes = lax.broadcasted_iota(jnp.int32, (1, 128), 1)

    def owner_at(f, j):
        return jnp.where(j < v.counts[0, f], lax.div(v.ids[f, 0, j], experts), -1)

    wanted = jnp.zeros((1, 128), jnp.int32)
    listed = jnp.zeros((1, 128), jnp.int32)
    spot = [jnp.full((1, 128), -1, jnp.int32) for _ in range(cap)]
    share_of = [jnp.zeros((1, 128), f32) for _ in range(cap)]
    for f in range(frames):
        hit = jnp.zeros((1, 128), jnp.int32)
        gate = jnp.zeros((1, 128), f32)
        for j in range(slots):
            here = lanes == owner_at(f, j)
            hit = jnp.where(here, 1, hit)
            gate = jnp.where(here, v.gates[f, 0, j], gate)
            wanted = jnp.where(here, lax.rem(v.ids[f, 0, j], experts), wanted)
        for c in range(cap):
            taken = jnp.logical_and(hit == 1, listed == c)
            spot[c] = jnp.where(taken, f, spot[c])
            share_of[c] = jnp.where(taken, gate, share_of[c])
        listed = listed + hit
    asked = jnp.concatenate(
        [wanted] + spot + [jnp.zeros((127 - cap, 128), jnp.int32)], axis=0
    )
    shares = jnp.concatenate(share_of + [jnp.zeros((128 - cap, 128), f32)], axis=0)
    asked, shares = jnp.transpose(asked), jnp.transpose(shares)
    for o in range(owners):
        v.note[o] = asked[o : o + 1]
        v.weight[o] = shares[o : o + 1]
    own_scalars = pltpu.make_async_copy(v.note, v.os, v.local_sem.at[4])
    own_scalars.start()

    pl.semaphore_wait(barrier, owners - 1 + tiles - 1)

    def along(act, s, zs, fr, co):
        up = jnp.logical_and(zs <= z, z < deep - 1)
        down = jnp.logical_and(zs >= z, z > 0)
        if fr is not None:
            pl.when(up)(
                lambda: act(
                    remote(fr, v.f.at[s, t], v.f_up.at[zs], v.f_recv.at[s], me + across, t)
                )
            )
            pl.when(down)(
                lambda: act(
                    remote(fr, v.f.at[s, t], v.f_down.at[zs], v.f_recv.at[s], me - across, t)
                )
            )
        if co is not None:
            pl.when(up)(
                lambda: act(remote(co, v.c.at[s], v.c_up.at[zs], v.c_recv.at[zs], me + across, t))
            )
            pl.when(down)(
                lambda: act(remote(co, v.c.at[s], v.c_down.at[zs], v.c_recv.at[zs], me - across, t))
            )

    def side_frames(act, s, zs, fr):
        for j in range(1, across):
            act(
                remote(
                    fr, v.f.at[s, t], v.f_side.at[j - 1, zs], v.f_recv.at[s],
                    z * across + lax.rem(x + j, across), t,
                )
            )

    def side_packed(act, s, zs):
        for j in range(1, across):
            act(
                remote(
                    v.cpo.at[j - 1, zs], v.cp.at[s], v.cp_send.at[j - 1, zs], v.cp_recv.at[s],
                    z * across + lax.rem(x + j, across), t,
                )
            )

    def near_rows(act, s, fr):
        pl.when(has_below)(
            lambda: act(
                remote(fr, v.f.at[s, t], v.near_send.at[0, s], v.ft_recv.at[s, t], me, t + 1)
            )
        )
        pl.when(has_above)(
            lambda: act(
                remote(fr, v.f.at[s, t], v.near_send.at[1, s], v.ft_recv.at[s, t], me, t - 1)
            )
        )

    def far_rows(act, s):
        for j in range(1, high):
            yy = lax.rem(y + j, high)
            beside = jnp.logical_or(
                jnp.logical_and(yy == y + 1, core == cores - 1),
                jnp.logical_and(yy == y - 1, core == 0),
            )
            pl.when(jnp.logical_not(beside))(
                lambda j=j, yy=yy: act(
                    remote(
                        v.f.at[s, t], v.f.at[s, t], v.far_send.at[j - 1, s], v.ft_recv.at[s, t],
                        me, yy * cores + core,
                    )
                )
            )

    def entering(body):
        for j in range(1, high):
            yy = lax.rem(y + j, high)
            for c in range(cores):
                across_low = jnp.logical_and(yy == y - 1, c == cores - 1)
                across_high = jnp.logical_and(yy == y + 1, c == 0)
                straight = jnp.logical_not(jnp.logical_or(across_low, across_high))
                enters = jnp.logical_or(
                    jnp.logical_and(across_low, core == 0),
                    jnp.logical_or(
                        jnp.logical_and(across_high, core == cores - 1),
                        jnp.logical_and(straight, core == c),
                    ),
                )
                body(j, c, yy * cores + c, enters, straight)

    def pass_on(act, s):
        def one(j, c, tt, enters, straight):
            @pl.when(enters)
            def _():
                for i in range(1, cores):
                    act(
                        remote(
                            v.f.at[s, tt], v.f.at[s, tt], v.pass_send.at[j - 1, c, i - 1, s],
                            v.ft_recv.at[s, tt], me, y * cores + lax.rem(core + i, cores),
                        )
                    )

        entering(one)

    def gather_far(s):
        def one(j, c, tt, enters, straight):
            pl.when(jnp.logical_and(enters, straight))(
                lambda: received(v.f.at[s, tt], v.ft_recv.at[s, tt])
            )

        entering(one)
        pass_on(go, s)

    def gather_passed(s):
        def one(j, c, tt, enters, straight):
            pl.when(jnp.logical_not(enters))(
                lambda: received(v.f.at[s, tt], v.ft_recv.at[s, tt])
            )

        entering(one)

    def edge_down(act, s):
        act(
            remote(
                v.eo.at[s, 1], v.above.at[s], v.above_send.at[s], v.above_recv.at[s], me, t + 1
            )
        )

    def edge_up(act, s):
        act(
            remote(
                v.eo.at[s, 0], v.below.at[s], v.below_send.at[s], v.below_recv.at[s], me, t - 1
            )
        )

    def slices(s):
        for j in range(1, tiles):
            tt = lax.rem(t + j, tiles)
            go(remote(v.go.at[s, tt], v.gi.at[s, t], v.g_send.at[s], v.g_recv.at[s], me, tt))

    def gates(s):
        go(remote(v.gate.at[s], v.gated.at[me], v.gate_send.at[0], v.gate_recv.at[0], s, t))

    def side_act(act, s, zs, xj):
        act(
            remote(
                v.act.at[s], v.sai.at[xj - 1, zs],
                v.sa_send.at[xj - 1, zs], v.sa_recv.at[xj - 1, zs],
                z * across + lax.rem(s, across), t,
            )
        )

    def side_back(act, s, zs, xj):
        act(
            remote(
                v.sbo.at[xj - 1, zs], v.sbi.at[xj - 1, zs],
                v.sb_send.at[xj - 1, zs], v.sb_recv.at[xj - 1, zs],
                z * across + lax.rem(s, across), t,
            )
        )

    def far_terms(act, zs, part):
        act(
            remote(
                v.fo.at[zs, part], v.fi.at[z, part],
                v.fo_send.at[part, zs], v.fi_recv.at[part, z], zs * across + x, t,
            )
        )

    def sent(ref, sem):
        remote(ref, ref, sem, v.spare_sem.at[0], me, t).wait_send()

    def received(ref, sem):
        remote(ref, ref, v.spare_sem.at[0], sem, me, t).wait_recv()

    def send_notes():
        for j in range(1, owners):
            peer = lax.rem(me + j, owners)
            go(
                remote(
                    v.note.at[pl.ds(lax.div(peer, across) * across, across)], v.n.at[me],
                    v.note_send.at[0], v.note_recv.at[0], peer, t,
                )
            )
            go(
                remote(
                    v.weight.at[peer], v.w.at[me],
                    v.note_send.at[1], v.note_recv.at[1], peer, t,
                )
            )

    send_notes()
    own_notes = pltpu.make_async_copy(
        v.note.at[pl.ds(z * across, across)], v.n.at[me], v.local_sem.at[1]
    )
    own_notes.start()
    own_weights = pltpu.make_async_copy(v.weight.at[me], v.w.at[me], v.local_sem.at[2])
    own_weights.start()
    own_rows.wait()
    along(go, me, z, v.f.at[me, t], None)
    side_frames(go, me, z, v.f.at[me, t])
    near_rows(go, me, v.f.at[me, t])
    own_cot.wait()
    along(go, me, z, None, v.c.at[me])

    def places(s, xo):
        return [v.ns[s, xo, 0, 1 + c] for c in range(cap)]

    def tile_places(tt, s):
        return [v.ts[tt, s, x, 0, 1 + c] for c in range(cap)]

    def picked(spots, load):
        parts = []
        for c in range(cap):
            value = jnp.zeros((columns, channels), bf16)
            for f in range(frames):
                value = jnp.where(spots[c] == f, load(f), value)
            parts.append(value)
        return parts

    def pack(s, zs, load, spots_of):
        for j in range(1, across):
            parts = picked(spots_of(lax.rem(x + j, across)), load)
            for c in range(cap):
                v.cpo[j - 1, zs, c] = parts[c]
        side_packed(go, s, zs)
        parts = picked(spots_of(x), load)
        for c in range(cap):
            v.cp[s, c] = parts[c]

    own_scalars.wait()
    pack(
        me, z, lambda f: v.c[me, f],
        lambda xo: [v.os[z * across + xo, 0, 1 + c] for c in range(cap)],
    )

    @pl.when(jnp.logical_not(has_above))
    def _():
        v.above[...] = jnp.zeros_like(v.above)

    @pl.when(jnp.logical_not(has_below))
    def _():
        v.below[...] = jnp.zeros_like(v.below)

    @pl.loop(0, experts)
    def _(k):
        grad_ref[k] = jnp.zeros_like(grad_ref[k])

    def tile_notes():
        for j in range(1, tiles):
            go(remote(v.n, v.tn.at[t], v.tn_send.at[0], v.tn_recv.at[0], me, lax.rem(t + j, tiles)))

    own_notes.wait()
    own_weights.wait()
    received(v.n.at[pl.ds(0, owners - 1)], v.note_recv.at[0])
    received(v.w.at[pl.ds(0, owners - 1)], v.note_recv.at[1])
    tile_notes()
    copies = [
        pltpu.make_async_copy(v.n, v.tn.at[t], v.local_sem.at[1]),
        pltpu.make_async_copy(v.n, v.ns, v.local_sem.at[2]),
        pltpu.make_async_copy(v.w, v.ws, v.local_sem.at[4]),
    ]
    for copy in copies:
        copy.start()
    for copy in copies:
        copy.wait()

    def settle():
        received(v.tn.at[pl.ds(0, tiles - 1)], v.tn_recv.at[0])
        tile_scalars = pltpu.make_async_copy(v.tn, v.ts, v.local_sem.at[1])
        tile_scalars.start()
        tile_scalars.wait()

    step = 2 * across
    count = (deep + 1) * step

    def stage(n, body, lead=None):
        k, slot = lax.div(n, step), lax.rem(n, step)
        sign, xj = lax.rem(slot, 2), lax.div(slot, 2)
        hops = k - lax.div(xj + across - 1, across)
        zs = z + hops * (2 * sign - 1)
        s = zs * across + lax.rem(x + xj, across)
        cond = jnp.logical_and(
            jnp.logical_and(n >= 0, n < count), jnp.logical_and(zs >= 0, zs < deep)
        )
        cond = jnp.logical_and(cond, jnp.logical_and(hops >= 0, hops + 1 - sign > 0))
        cond = jnp.logical_and(cond, hops < deep)
        if lead is True:
            cond = jnp.logical_and(cond, jnp.logical_and(xj == 0, n > 0))
        elif lead is False:
            cond = jnp.logical_and(cond, xj > 0)
        pl.when(cond)(lambda: body(s, zs, xj))

    def arrive(s, zs, xj):
        received(v.f.at[s, t], v.f_recv.at[s])

        @pl.when(xj == 0)
        def _():
            along(go, s, zs, v.f.at[s, t], None)
            side_frames(go, s, zs, v.f.at[s, t])

        near_rows(go, s, v.f.at[s, t])

        @pl.when(xj == 0)
        def _():
            received(v.c.at[s], v.c_recv.at[zs])
            along(go, s, zs, None, v.c.at[s])
            pack(s, zs, lambda f: v.c[s, f], lambda xo: places(s, xo))

        @pl.when(xj > 0)
        def _():
            received(v.cp.at[s], v.cp_recv.at[s])

    place = lax.broadcasted_iota(jnp.int32, (rows, 1), 0)
    item = place // columns
    column = place % columns

    def later(value):
        return jnp.where(column == 0, 0.0, pltpu.roll(value, 1, 0))

    def sooner(value):
        return jnp.where(column == columns - 1, 0.0, pltpu.roll(value, rows - 1, 0))

    def compute(s, zs, xj):
        pl.when(has_above)(lambda: received(v.f.at[s, t_above], v.ft_recv.at[s, t_above]))
        pl.when(has_below)(lambda: received(v.f.at[s, t_below], v.ft_recv.at[s, t_below]))
        e = v.ns[s, x, 0, 0]
        spots = places(s, x)
        blank = jnp.zeros((rows, channels), bf16)

        def gather(tt):
            return jnp.concatenate(picked(spots, lambda f: v.f[s, tt, f]), axis=0)

        window = [
            jnp.where(has_above, gather(t_above), blank),
            gather(t),
            jnp.where(has_below, gather(t_below), blank),
        ]
        upstream = v.cp[s].reshape(rows, channels).astype(f32)
        weight = jnp.zeros((rows, 1), f32)
        for c in range(cap):
            weight = jnp.where(item == c, v.ws[s, 0, c], weight)

        def column_term(db):
            total = jnp.dot(window[0], v.bank[e, db], preferred_element_type=f32)
            for da in (1, 2):
                total = total + jnp.dot(
                    window[da], v.bank[e, 3 * da + db], preferred_element_type=f32
                )
            return total

        pre = column_term(1) + later(column_term(0)) + sooner(column_term(2))
        pre = pre.astype(bf16).astype(f32)
        squash = jax.nn.sigmoid(pre)
        activated = pre * squash
        slope = squash * (1.0 + pre * (1.0 - squash))
        v.act[s] = (weight * activated).astype(bf16).reshape(cap, columns, channels)
        pl.when(xj > 0)(lambda: side_act(go, s, zs, xj))
        sums = jnp.sum((upstream * activated).reshape(cap, columns, channels), axis=1)
        sums = jnp.broadcast_to(jnp.sum(sums, axis=1, keepdims=True), (cap, 128))
        sums = jnp.concatenate([sums, jnp.zeros((8 - cap, 128), f32)], axis=0)
        v.gate[s] = sums

        @pl.when(s != me)
        def _():
            gates(s)

        @pl.when(s == me)
        def _():
            v.gated[me] = sums

        grad = (upstream * weight * slope).astype(bf16)
        turned = jnp.transpose(grad.astype(f32)).astype(bf16)
        for k in range(tiles):
            v.go[s, k] = turned[k * share : (k + 1) * share]
        v.gi[s, t] = v.go[s, t]
        slices(s)
        for da in (0, 2, 1):
            parts = [
                lax.dot_general(
                    grad,
                    v.bank[e, 3 * da + db],
                    (((1,), (1,)), ((), ())),
                    preferred_element_type=f32,
                )
                for db in range(3)
            ]
            total = parts[1] + sooner(parts[0]) + later(parts[2])
            total = total.astype(bf16).reshape(cap, columns, channels)
            if da == 1:
                v.bk[s] = total
            else:
                v.eo[s, da // 2] = total
        pl.when(has_above)(lambda: edge_up(go, s))
        pl.when(has_below)(lambda: edge_down(go, s))

    def rims(s):
        pl.when(has_above)(lambda: received(v.above.at[s], v.above_recv.at[s]))
        pl.when(has_below)(lambda: received(v.below.at[s], v.below_recv.at[s]))

    def spread_out(value, spots, load, f):
        found = jnp.zeros((columns, channels), bf16)
        for c in range(cap):
            found = jnp.where(spots[c] == f, load(c), found)
        return value + found.astype(f32)

    def back_rows(s):
        mine = places(s, x)
        upper = [jnp.where(has_above, p, -1) for p in tile_places(t_above, s)]
        lower = [jnp.where(has_below, p, -1) for p in tile_places(t_below, s)]

        def row(f):
            value = jnp.zeros((columns, channels), f32)
            value = spread_out(value, mine, lambda c: v.bk[s, c], f)
            value = spread_out(value, upper, lambda c: v.above[s, c], f)
            return spread_out(value, lower, lambda c: v.below[s, c], f)

        return row

    def to_side(s, zs, xj):
        rims(s)
        row = back_rows(s)
        for f in range(frames):
            v.sbo[xj - 1, zs, f] = row(f).astype(bf16)
        side_back(go, s, zs, xj)

    def far_act(s, zs, xj):
        for j in range(1, across):
            received(v.sai.at[j - 1, zs], v.sa_recv.at[j - 1, zs])
        spots = [places(s, x)] + [
            places(s, lax.rem(x + across - j, across)) for j in range(1, across)
        ]
        for f in range(frames):
            value = spread_out(
                jnp.zeros((columns, channels), f32), spots[0], lambda c: v.act[s, c], f
            )
            for j in range(1, across):
                value = spread_out(value, spots[j], lambda c: v.sai[j - 1, zs, c], f)
            v.total[1, f] = value

        @pl.when(zs == z)
        def _():
            for f in range(frames):
                v.base[1, f] = v.total[1, f] + v.f[me, t, f].astype(f32)

        @pl.when(zs != z)
        def _():
            v.fo[zs, 1] = v.total[1].astype(bf16)
            far_terms(go, zs, 1)

    def far_back(s, zs, xj):
        rims(s)
        for j in range(1, across):
            received(v.sbi.at[j - 1, zs], v.sb_recv.at[j - 1, zs])
        row = back_rows(s)
        for f in range(frames):
            value = row(f)
            for j in range(1, across):
                value = value + v.sbi[j - 1, zs, f].astype(f32)
            v.total[0, f] = value

        @pl.when(zs == z)
        def _():
            for f in range(frames):
                v.base[0, f] = v.total[0, f] + v.c[me, f].astype(f32)

        @pl.when(zs != z)
        def _():
            v.fo[zs, 0] = v.total[0].astype(bf16)
            far_terms(go, zs, 0)

    lane = lax.broadcasted_iota(jnp.int32, (1, rows), 1) % columns

    def weigh(s, zs, xj):
        gather_passed(s)
        received(v.gi.at[s, pl.ds(0, tiles - 1)], v.g_recv.at[s])
        for tt in range(tiles):
            e = v.ts[tt, s, x, 0, 0]
            spots = tile_places(tt, s)
            span = slice(tt * rows, (tt + 1) * rows)
            for da in range(3):
                source = tt + da - 1
                if 0 <= source < tiles:
                    parts = picked(spots, lambda f: v.f[s, source, f])
                    v.xw[da, span] = jnp.concatenate(parts, axis=0)
                else:
                    v.xw[da, span] = jnp.zeros((rows, channels), bf16)
            g = v.gi[s, tt].astype(f32)
            moved = [
                jnp.where(lane == columns - 1, 0.0, pltpu.roll(g, rows - 1, 1)).astype(bf16),
                v.gi[s, tt],
                jnp.where(lane == 0, 0.0, pltpu.roll(g, 1, 1)).astype(bf16),
            ]
            for db in range(3):
                for k in range(experts):
                    first = (db * experts + k) * share
                    v.gt[first : first + share, span] = jnp.where(
                        e == k, moved[db], jnp.zeros_like(moved[db])
                    )
        for da in range(3):
            term = jnp.dot(v.gt[...], v.xw[da], preferred_element_type=f32)
            term = term.reshape(3, experts, share, channels)
            for db in range(3):
                grad_ref[:, 3 * da + db] += term[db]

    @pl.loop(0, count + count)
    def _(n):
        pl.when(n == step)(load_bank.wait)
        pl.when(n == (step + 3))(settle)
        stage(n - step, compute)
        stage(n - (step + 3), to_side, lead=False)
        stage(n - 4 * step, far_act, lead=True)
        stage(n - count, far_back, lead=True)
        stage(n - count, lambda s, zs, xj: far_rows(go, s))
        pl.when(n > 1)(lambda: stage(n, arrive))

    @pl.loop(0, count + 2)
    def _(n):
        stage(n, lambda s, zs, xj: gather_far(s))
        stage(n - 2, weigh)

    some = pl.ds(0, owners - 1)
    received(v.gated.at[some], v.gate_recv.at[0])
    sent(v.gate.at[some], v.gate_send.at[0])
    for f in range(frames):
        at = jnp.full((1, 128), -1, jnp.int32)
        for j in range(slots):
            at = jnp.where(lanes == j, owner_at(f, j), at)
        found = jnp.zeros((1, 128), f32)
        for o in range(owners):
            for c in range(cap):
                owner = jnp.where(v.os[o, 0, 1 + c] == f, o, -2)
                found = jnp.where(at == owner, v.gated[o, c : c + 1], found)
        gate_ref[f] = found[:, :slots]
    sent(v.n.at[some], v.note_send.at[0])
    sent(v.w.at[some], v.note_send.at[1])
    sent(v.tn.at[pl.ds(0, tiles - 1)], v.tn_send.at[0])

    def finish(s, zs, xj):
        @pl.when(xj == 0)
        def _():
            along(drain, s, zs, v.f.at[s, t], v.c.at[s])
            side_frames(drain, s, zs, v.f.at[s, t])
            side_packed(drain, s, zs)
            for part in range(2):
                pl.when(zs != z)(lambda part=part: far_terms(drain, zs, part))

        @pl.when(xj > 0)
        def _():
            side_act(drain, s, zs, xj)
            side_back(drain, s, zs, xj)

        near_rows(drain, s, v.f.at[s, t])
        far_rows(drain, s)
        pass_on(drain, s)
        sent(v.go.at[s, pl.ds(0, tiles - 1)], v.g_send.at[s])
        pl.when(has_above)(lambda: edge_up(drain, s))
        pl.when(has_below)(lambda: edge_down(drain, s))

    @pl.loop(0, count)
    def _(n):
        stage(n, finish)

    far_act(me, z, 0)
    far_back(me, z, 0)
    for k in range(1, deep):
        zs = lax.rem(z + k, deep)
        for part in range(2):
            received(v.fi.at[zs, part], v.fi_recv.at[part, zs])
    for f in range(frames):
        first, second = v.base[0, f], v.base[1, f]
        for k in range(1, deep):
            zs = lax.rem(z + k, deep)
            first = first + v.fi[zs, 0, f].astype(f32)
            second = second + v.fi[zs, 1, f].astype(f32)
        input_ref[f] = first.astype(bf16)
        result_ref[f] = second.astype(bf16)


def layer(frames, cot, ids, counts, gates, kernels, owners, tiles):
    deep, across = grid_of(owners)
    cores = 1 if tiles % 2 else 2
    high = tiles // cores
    count, columns, channels = frames.shape
    experts, taps, _, outputs = kernels.shape
    share = outputs // tiles
    cap = CAP
    rows = cap * columns
    dma = pltpu.SemaphoreType.DMA
    vmem, hbm = pl.BlockSpec(memory_space=pltpu.VMEM), pl.BlockSpec(memory_space=pltpu.HBM)
    bf16, f32, i32 = jnp.bfloat16, jnp.float32, jnp.int32
    beside, mates, far = (max(value - 1, 1) for value in (across, cores, high))
    scratch = dict(
        f=pltpu.VMEM((owners, tiles, count, columns, channels), bf16),
        c=pltpu.VMEM((owners, count, columns, channels), bf16),
        cp=pltpu.VMEM((owners, cap, columns, channels), bf16),
        cpo=pltpu.VMEM((beside, deep, cap, columns, channels), bf16),
        n=pltpu.VMEM((owners, across, 1, 128), i32),
        w=pltpu.VMEM((owners, 1, 128), f32),
        tn=pltpu.VMEM((tiles, owners, across, 1, 128), i32),
        os=pltpu.SMEM((owners, 1, 128), i32),
        ns=pltpu.SMEM((owners, across, 1, 128), i32),
        ws=pltpu.SMEM((owners, 1, 128), f32),
        ts=pltpu.SMEM((tiles, owners, across, 1, 128), i32),
        bank=pltpu.VMEM(kernels.shape, bf16),
        act=pltpu.VMEM((owners, cap, columns, channels), bf16),
        bk=pltpu.VMEM((owners, cap, columns, channels), bf16),
        eo=pltpu.VMEM((owners, 2, cap, columns, channels), bf16),
        above=pltpu.VMEM((owners, cap, columns, channels), bf16),
        below=pltpu.VMEM((owners, cap, columns, channels), bf16),
        go=pltpu.VMEM((owners, tiles, share, rows), bf16),
        gi=pltpu.VMEM((owners, tiles, share, rows), bf16),
        gate=pltpu.VMEM((owners, 8, 128), f32),
        gated=pltpu.VMEM((owners, 8, 128), f32),
        ids=pltpu.SMEM(ids.shape, i32),
        counts=pltpu.SMEM(counts.shape, i32),
        gates=pltpu.SMEM(gates.shape, f32),
        note=pltpu.VMEM((owners, 1, 128), i32),
        weight=pltpu.VMEM((owners, 1, 128), f32),
        sbo=pltpu.VMEM((beside, deep, count, columns, channels), bf16),
        sbi=pltpu.VMEM((beside, deep, count, columns, channels), bf16),
        sai=pltpu.VMEM((beside, deep, cap, columns, channels), bf16),
        fo=pltpu.VMEM((deep, 2, count, columns, channels), bf16),
        fi=pltpu.VMEM((deep, 2, count, columns, channels), bf16),
        total=pltpu.VMEM((2, count, columns, channels), f32),
        base=pltpu.VMEM((2, count, columns, channels), f32),
        xw=pltpu.VMEM((3, tiles * rows, channels), bf16),
        gt=pltpu.VMEM((3 * experts * share, tiles * rows), bf16),
        local_sem=dma((6,)),
        spare_sem=dma((1,)),
        note_send=dma((2,)), note_recv=dma((2,)),
        tn_send=dma((1,)), tn_recv=dma((1,)),
        f_up=dma((deep,)), f_down=dma((deep,)), f_side=dma((beside, deep)), f_recv=dma((owners,)),
        c_up=dma((deep,)), c_down=dma((deep,)), c_recv=dma((deep,)),
        cp_send=dma((beside, deep)), cp_recv=dma((owners,)),
        near_send=dma((2, owners)), far_send=dma((far, owners)),
        pass_send=dma((far, cores, mates, owners)), ft_recv=dma((owners, tiles)),
        above_send=dma((owners,)), above_recv=dma((owners,)),
        below_send=dma((owners,)), below_recv=dma((owners,)),
        g_send=dma((owners,)), g_recv=dma((owners,)),
        gate_send=dma((1,)), gate_recv=dma((1,)),
        sb_send=dma((beside, deep)), sb_recv=dma((beside, deep)),
        sa_send=dma((beside, deep)), sa_recv=dma((beside, deep)),
        fo_send=dma((2, deep)), fi_recv=dma((2, deep)),
    )
    held = 2 * frames.size * 4 * 2 + experts * taps * share * channels * 4 + owners * 8 * 128 * 4
    for ref in scratch.values():
        if ref.memory_space == pltpu.VMEM:
            held += math.prod(ref.shape) * jnp.dtype(ref.dtype).itemsize
    return pl.pallas_call(
        functools.partial(layer_kernel, deep, across, high, cores, tuple(scratch)),
        out_shape=[
            jax.ShapeDtypeStruct(frames.shape, bf16),
            jax.ShapeDtypeStruct(frames.shape, bf16),
            jax.ShapeDtypeStruct(gates.shape, f32),
            jax.ShapeDtypeStruct((experts, taps, share, channels), f32),
        ],
        in_specs=[hbm] * 6,
        out_specs=[vmem] * 4,
        scratch_shapes=list(scratch.values()),
        compiler_params=pltpu.CompilerParams(
            collective_id=0, has_side_effects=True, vmem_limit_bytes=held + (8 << 20)
        ),
        name="layer",
    )(
        *(
            pltpu.with_memory_space_constraint(value, pltpu.HBM)
            for value in (frames, cot, ids, counts, gates, kernels)
        )
    )


def settle_kernel(count, *refs):
    sems = refs[2 * count]
    copies = [
        pltpu.make_async_copy(refs[i], refs[count + i], sems.at[i]) for i in range(count)
    ]
    for copy in copies:
        copy.start()
    for copy in copies:
        copy.wait()


def settled(*arrays):
    count = len(arrays)
    anywhere = pl.BlockSpec(memory_space=pl.ANY)
    return pl.pallas_call(
        functools.partial(settle_kernel, count),
        out_shape=[jax.ShapeDtypeStruct(a.shape, a.dtype) for a in arrays],
        in_specs=[anywhere] * count,
        out_specs=[pl.BlockSpec(memory_space=pltpu.HBM)] * count,
        scratch_shapes=[pltpu.SemaphoreType.DMA((count,))],
        compiler_params=pltpu.CompilerParams(vmem_limit_bytes=1 << 20),
        name="settled",
    )(*arrays)


def shards(frames, kernels, experts, counts, gate_weights, cotangent):
    owners = lax.axis_size("dp")
    tiles = lax.axis_size("tile")
    result, input_grad, gate_grad, kernel_part = settled(
        *layer(
            frames[:, 0], cotangent[:, 0], experts, counts.T, gate_weights, kernels, owners, tiles
        )
    )
    kernel_part = jnp.swapaxes(kernel_part, 2, 3)
    return (result[:, None], input_grad[:, None], gate_grad, kernel_part)


def solution(mesh):
    return jax.shard_map(
        shards,
        mesh=mesh,
        in_specs=(
            P("dp", "tile", None, None),
            P("dp", None, None, None),
            P("dp", "tile", None),
            P("dp", "tile"),
            P("dp", "tile", None),
            P("dp", "tile", None, None),
        ),
        out_specs=(
            P("dp", "tile", None, None),
            P("dp", "tile", None, None),
            P("dp", "tile", None),
            P("dp", None, None, "tile"),
        ),
        check_vma=False,
    )
```

```python
import functools
import math
from types import SimpleNamespace

import jax
import jax.numpy as jnp
from jax import lax
from jax.experimental import pallas as pl
from jax.experimental.pallas import tpu as pltpu
from jax.sharding import PartitionSpec as P

CAP = 2


def grid_of(owners):
    across = 1
    while across * across * 4 <= owners:
        across *= 2
    while owners % across:
        across -= 1
    return owners // across, across


def remote(src, dst, send, recv, dp, tile):
    return pltpu.make_async_remote_copy(
        src_ref=src,
        dst_ref=dst,
        send_sem=send,
        recv_sem=recv,
        device_id=(dp, tile),
        device_id_type=pl.DeviceIdType.MESH,
    )


def go(copy):
    copy.start()


def drain(copy):
    copy.wait_send()


def layer_kernel(
    deep, across, high, cores, names,
    frames_hbm, cot_hbm, ids_hbm, counts_hbm, gates_hbm, bank_hbm,
    result_ref, input_ref, gate_ref, grad_ref, *rest,
):
    v = SimpleNamespace(**dict(zip(names, rest)))
    me, t = lax.axis_index("dp"), lax.axis_index("tile")
    z, x = lax.div(me, across), lax.rem(me, across)
    y, core = lax.div(t, cores), lax.rem(t, cores)
    owners, tiles = deep * across, high * cores
    _, _, frames, columns, channels = v.f.shape
    experts, taps, share, _ = grad_ref.shape
    cap = CAP
    rows = cap * columns
    has_above, has_below = t > 0, t < tiles - 1
    t_above, t_below = t - has_above.astype(jnp.int32), t + has_below.astype(jnp.int32)
    bf16, f32 = jnp.bfloat16, jnp.float32

    load_bank = pltpu.make_async_copy(bank_hbm, v.bank, v.local_sem.at[0])
    lists = [
        pltpu.make_async_copy(ids_hbm, v.ids, v.local_sem.at[1]),
        pltpu.make_async_copy(counts_hbm, v.counts, v.local_sem.at[2]),
        pltpu.make_async_copy(gates_hbm, v.gates, v.local_sem.at[4]),
    ]
    for copy in lists:
        copy.start()
    own_rows = pltpu.make_async_copy(frames_hbm, v.f.at[me, t], v.local_sem.at[3])
    own_rows.start()
    own_cot = pltpu.make_async_copy(cot_hbm, v.c.at[me], v.local_sem.at[5])
    own_cot.start()
    load_bank.start()

    barrier = pltpu.get_barrier_semaphore()
    for j in range(1, owners):
        pl.semaphore_signal(
            barrier, device_id=(lax.rem(me + j, owners), t), device_id_type=pl.DeviceIdType.MESH
        )
    for j in range(1, tiles):
        pl.semaphore_signal(
            barrier, device_id=(me, lax.rem(t + j, tiles)), device_id_type=pl.DeviceIdType.MESH
        )

    for copy in lists:
        copy.wait()
    slots = v.ids.shape[2]
    lanes = lax.broadcasted_iota(jnp.int32, (1, 128), 1)

    def owner_at(f, j):
        return jnp.where(j < v.counts[0, f], lax.div(v.ids[f, 0, j], experts), -1)

    wanted = jnp.zeros((1, 128), jnp.int32)
    listed = jnp.zeros((1, 128), jnp.int32)
    spot = [jnp.full((1, 128), -1, jnp.int32) for _ in range(cap)]
    share_of = [jnp.zeros((1, 128), f32) for _ in range(cap)]
    for f in range(frames):
        hit = jnp.zeros((1, 128), jnp.int32)
        gate = jnp.zeros((1, 128), f32)
        for j in range(slots):
            here = lanes == owner_at(f, j)
            hit = jnp.where(here, 1, hit)
            gate = jnp.where(here, v.gates[f, 0, j], gate)
            wanted = jnp.where(here, lax.rem(v.ids[f, 0, j], experts), wanted)
        for c in range(cap):
            taken = jnp.logical_and(hit == 1, listed == c)
            spot[c] = jnp.where(taken, f, spot[c])
            share_of[c] = jnp.where(taken, gate, share_of[c])
        listed = listed + hit
    asked = jnp.concatenate(
        [wanted] + spot + [jnp.zeros((127 - cap, 128), jnp.int32)], axis=0
    )
    shares = jnp.concatenate(share_of + [jnp.zeros((128 - cap, 128), f32)], axis=0)
    asked, shares = jnp.transpose(asked), jnp.transpose(shares)
    for o in range(owners):
        v.note[o] = asked[o : o + 1]
        v.weight[o] = shares[o : o + 1]
    own_scalars = pltpu.make_async_copy(v.note, v.os, v.local_sem.at[4])
    own_scalars.start()

    pl.semaphore_wait(barrier, owners - 1 + tiles - 1)

    def along(act, s, zs, fr, co):
        up = jnp.logical_and(zs <= z, z < deep - 1)
        down = jnp.logical_and(zs >= z, z > 0)
        if fr is not None:
            pl.when(up)(
                lambda: act(
                    remote(fr, v.f.at[s, t], v.f_up.at[zs], v.f_recv.at[s], me + across, t)
                )
            )
            pl.when(down)(
                lambda: act(
                    remote(fr, v.f.at[s, t], v.f_down.at[zs], v.f_recv.at[s], me - across, t)
                )
            )
        if co is not None:
            pl.when(up)(
                lambda: act(remote(co, v.c.at[s], v.c_up.at[zs], v.c_recv.at[zs], me + across, t))
            )
            pl.when(down)(
                lambda: act(remote(co, v.c.at[s], v.c_down.at[zs], v.c_recv.at[zs], me - across, t))
            )

    def side_frames(act, s, zs, fr):
        for j in range(1, across):
            act(
                remote(
                    fr, v.f.at[s, t], v.f_side.at[j - 1, zs], v.f_recv.at[s],
                    z * across + lax.rem(x + j, across), t,
                )
            )

    def side_packed(act, s, zs):
        for j in range(1, across):
            act(
                remote(
                    v.cpo.at[j - 1, zs], v.cp.at[s], v.cp_send.at[j - 1, zs], v.cp_recv.at[s],
                    z * across + lax.rem(x + j, across), t,
                )
            )

    def near_rows(act, s, fr):
        pl.when(has_below)(
            lambda: act(
                remote(fr, v.f.at[s, t], v.near_send.at[0, s], v.ft_recv.at[s, t], me, t + 1)
            )
        )
        pl.when(has_above)(
            lambda: act(
                remote(fr, v.f.at[s, t], v.near_send.at[1, s], v.ft_recv.at[s, t], me, t - 1)
            )
        )

    def far_rows(act, s):
        for j in range(1, high):
            yy = lax.rem(y + j, high)
            beside = jnp.logical_or(
                jnp.logical_and(yy == y + 1, core == cores - 1),
                jnp.logical_and(yy == y - 1, core == 0),
            )
            pl.when(jnp.logical_not(beside))(
                lambda j=j, yy=yy: act(
                    remote(
                        v.f.at[s, t], v.f.at[s, t], v.far_send.at[j - 1, s], v.ft_recv.at[s, t],
                        me, yy * cores + core,
                    )
                )
            )

    def entering(body):
        for j in range(1, high):
            yy = lax.rem(y + j, high)
            for c in range(cores):
                across_low = jnp.logical_and(yy == y - 1, c == cores - 1)
                across_high = jnp.logical_and(yy == y + 1, c == 0)
                straight = jnp.logical_not(jnp.logical_or(across_low, across_high))
                enters = jnp.logical_or(
                    jnp.logical_and(across_low, core == 0),
                    jnp.logical_or(
                        jnp.logical_and(across_high, core == cores - 1),
                        jnp.logical_and(straight, core == c),
                    ),
                )
                body(j, c, yy * cores + c, enters, straight)

    def pass_on(act, s):
        def one(j, c, tt, enters, straight):
            @pl.when(enters)
            def _():
                for i in range(1, cores):
                    act(
                        remote(
                            v.f.at[s, tt], v.f.at[s, tt], v.pass_send.at[j - 1, c, i - 1, s],
                            v.ft_recv.at[s, tt], me, y * cores + lax.rem(core + i, cores),
                        )
                    )

        entering(one)

    def gather_far(s):
        def one(j, c, tt, enters, straight):
            pl.when(jnp.logical_and(enters, straight))(
                lambda: received(v.f.at[s, tt], v.ft_recv.at[s, tt])
            )

        entering(one)
        pass_on(go, s)

    def gather_passed(s):
        def one(j, c, tt, enters, straight):
            pl.when(jnp.logical_not(enters))(
                lambda: received(v.f.at[s, tt], v.ft_recv.at[s, tt])
            )

        entering(one)

    def edge_down(act, s):
        act(
            remote(
                v.eo.at[s, 1], v.above.at[s], v.above_send.at[s], v.above_recv.at[s], me, t + 1
            )
        )

    def edge_up(act, s):
        act(
            remote(
                v.eo.at[s, 0], v.below.at[s], v.below_send.at[s], v.below_recv.at[s], me, t - 1
            )
        )

    def slices(s):
        for j in range(1, tiles):
            tt = lax.rem(t + j, tiles)
            go(remote(v.go.at[s, tt], v.gi.at[s, t], v.g_send.at[s], v.g_recv.at[s], me, tt))

    def gates(s):
        go(remote(v.gate.at[s], v.gated.at[me], v.gate_send.at[0], v.gate_recv.at[0], s, t))

    def side_act(act, s, zs, xj):
        act(
            remote(
                v.act.at[s], v.sai.at[xj - 1, zs],
                v.sa_send.at[xj - 1, zs], v.sa_recv.at[xj - 1, zs],
                z * across + lax.rem(s, across), t,
            )
        )

    def side_back(act, s, zs, xj):
        act(
            remote(
                v.sbo.at[xj - 1, zs], v.sbi.at[xj - 1, zs],
                v.sb_send.at[xj - 1, zs], v.sb_recv.at[xj - 1, zs],
                z * across + lax.rem(s, across), t,
            )
        )

    def far_terms(act, zs, part):
        act(
            remote(
                v.fo.at[zs, part], v.fi.at[z, part],
                v.fo_send.at[part, zs], v.fi_recv.at[part, z], zs * across + x, t,
            )
        )

    def sent(ref, sem):
        remote(ref, ref, sem, v.spare_sem.at[0], me, t).wait_send()

    def received(ref, sem):
        remote(ref, ref, v.spare_sem.at[0], sem, me, t).wait_recv()

    def send_notes():
        for j in range(1, owners):
            peer = lax.rem(me + j, owners)
            go(
                remote(
                    v.note.at[pl.ds(lax.div(peer, across) * across, across)], v.n.at[me],
                    v.note_send.at[0], v.note_recv.at[0], peer, t,
                )
            )
            go(
                remote(
                    v.weight.at[peer], v.w.at[me],
                    v.note_send.at[1], v.note_recv.at[1], peer, t,
                )
            )

    send_notes()
    own_notes = pltpu.make_async_copy(
        v.note.at[pl.ds(z * across, across)], v.n.at[me], v.local_sem.at[1]
    )
    own_notes.start()
    own_weights = pltpu.make_async_copy(v.weight.at[me], v.w.at[me], v.local_sem.at[2])
    own_weights.start()
    own_rows.wait()
    along(go, me, z, v.f.at[me, t], None)
    side_frames(go, me, z, v.f.at[me, t])
    near_rows(go, me, v.f.at[me, t])
    own_cot.wait()
    along(go, me, z, None, v.c.at[me])

    def places(s, xo):
        return [v.ns[s, xo, 0, 1 + c] for c in range(cap)]

    def tile_places(tt, s):
        return [v.ts[tt, s, x, 0, 1 + c] for c in range(cap)]

    def picked(spots, load):
        parts = []
        for c in range(cap):
            value = jnp.zeros((columns, channels), bf16)
            for f in range(frames):
                value = jnp.where(spots[c] == f, load(f), value)
            parts.append(value)
        return parts

    def pack(s, zs, load, spots_of):
        for j in range(1, across):
            parts = picked(spots_of(lax.rem(x + j, across)), load)
            for c in range(cap):
                v.cpo[j - 1, zs, c] = parts[c]
        side_packed(go, s, zs)
        parts = picked(spots_of(x), load)
        for c in range(cap):
            v.cp[s, c] = parts[c]

    own_scalars.wait()
    pack(
        me, z, lambda f: v.c[me, f],
        lambda xo: [v.os[z * across + xo, 0, 1 + c] for c in range(cap)],
    )

    @pl.when(jnp.logical_not(has_above))
    def _():
        v.above[...] = jnp.zeros_like(v.above)

    @pl.when(jnp.logical_not(has_below))
    def _():
        v.below[...] = jnp.zeros_like(v.below)

    @pl.loop(0, experts)
    def _(k):
        grad_ref[k] = jnp.zeros_like(grad_ref[k])

    def tile_notes():
        for j in range(1, tiles):
            go(remote(v.n, v.tn.at[t], v.tn_send.at[0], v.tn_recv.at[0], me, lax.rem(t + j, tiles)))

    own_notes.wait()
    own_weights.wait()
    received(v.n.at[pl.ds(0, owners - 1)], v.note_recv.at[0])
    received(v.w.at[pl.ds(0, owners - 1)], v.note_recv.at[1])
    tile_notes()
    copies = [
        pltpu.make_async_copy(v.n, v.tn.at[t], v.local_sem.at[1]),
        pltpu.make_async_copy(v.n, v.ns, v.local_sem.at[2]),
        pltpu.make_async_copy(v.w, v.ws, v.local_sem.at[4]),
    ]
    for copy in copies:
        copy.start()
    for copy in copies:
        copy.wait()

    def settle():
        received(v.tn.at[pl.ds(0, tiles - 1)], v.tn_recv.at[0])
        tile_scalars = pltpu.make_async_copy(v.tn, v.ts, v.local_sem.at[1])
        tile_scalars.start()
        tile_scalars.wait()

    step = 2 * across
    count = (deep + 1) * step

    def stage(n, body, lead=None):
        k, slot = lax.div(n, step), lax.rem(n, step)
        sign, xj = lax.rem(slot, 2), lax.div(slot, 2)
        hops = k - lax.div(xj + across - 1, across)
        zs = z + hops * (2 * sign - 1)
        s = zs * across + lax.rem(x + xj, across)
        cond = jnp.logical_and(
            jnp.logical_and(n >= 0, n < count), jnp.logical_and(zs >= 0, zs < deep)
        )
        cond = jnp.logical_and(cond, jnp.logical_and(hops >= 0, hops + 1 - sign > 0))
        cond = jnp.logical_and(cond, hops < deep)
        if lead is True:
            cond = jnp.logical_and(cond, jnp.logical_and(xj == 0, n > 0))
        elif lead is False:
            cond = jnp.logical_and(cond, xj > 0)
        pl.when(cond)(lambda: body(s, zs, xj))

    def arrive(s, zs, xj):
        received(v.f.at[s, t], v.f_recv.at[s])

        @pl.when(xj == 0)
        def _():
            along(go, s, zs, v.f.at[s, t], None)
            side_frames(go, s, zs, v.f.at[s, t])

        near_rows(go, s, v.f.at[s, t])

        @pl.when(xj == 0)
        def _():
            received(v.c.at[s], v.c_recv.at[zs])
            along(go, s, zs, None, v.c.at[s])
            pack(s, zs, lambda f: v.c[s, f], lambda xo: places(s, xo))

        @pl.when(xj > 0)
        def _():
            received(v.cp.at[s], v.cp_recv.at[s])

    place = lax.broadcasted_iota(jnp.int32, (rows, 1), 0)
    item = place // columns
    column = place % columns

    def later(value):
        return jnp.where(column == 0, 0.0, pltpu.roll(value, 1, 0))

    def sooner(value):
        return jnp.where(column == columns - 1, 0.0, pltpu.roll(value, rows - 1, 0))

    def compute(s, zs, xj):
        pl.when(has_above)(lambda: received(v.f.at[s, t_above], v.ft_recv.at[s, t_above]))
        pl.when(has_below)(lambda: received(v.f.at[s, t_below], v.ft_recv.at[s, t_below]))
        e = v.ns[s, x, 0, 0]
        spots = places(s, x)
        blank = jnp.zeros((rows, channels), bf16)

        def gather(tt):
            return jnp.concatenate(picked(spots, lambda f: v.f[s, tt, f]), axis=0)

        window = [
            jnp.where(has_above, gather(t_above), blank),
            gather(t),
            jnp.where(has_below, gather(t_below), blank),
        ]
        upstream = v.cp[s].reshape(rows, channels).astype(f32)
        weight = jnp.zeros((rows, 1), f32)
        for c in range(cap):
            weight = jnp.where(item == c, v.ws[s, 0, c], weight)

        def column_term(db):
            total = jnp.dot(window[0], v.bank[e, db], preferred_element_type=f32)
            for da in (1, 2):
                total = total + jnp.dot(
                    window[da], v.bank[e, 3 * da + db], preferred_element_type=f32
                )
            return total

        pre = column_term(1) + later(column_term(0)) + sooner(column_term(2))
        pre = pre.astype(bf16).astype(f32)
        squash = jax.nn.sigmoid(pre)
        activated = pre * squash
        slope = squash * (1.0 + pre * (1.0 - squash))
        v.act[s] = (weight * activated).astype(bf16).reshape(cap, columns, channels)
        pl.when(xj > 0)(lambda: side_act(go, s, zs, xj))
        sums = jnp.sum((upstream * activated).reshape(cap, columns, channels), axis=1)
        sums = jnp.broadcast_to(jnp.sum(sums, axis=1, keepdims=True), (cap, 128))
        sums = jnp.concatenate([sums, jnp.zeros((8 - cap, 128), f32)], axis=0)
        v.gate[s] = sums

        @pl.when(s != me)
        def _():
            gates(s)

        @pl.when(s == me)
        def _():
            v.gated[me] = sums

        grad = (upstream * weight * slope).astype(bf16)
        turned = jnp.transpose(grad.astype(f32)).astype(bf16)
        for k in range(tiles):
            v.go[s, k] = turned[k * share : (k + 1) * share]
        v.gi[s, t] = v.go[s, t]
        slices(s)
        for da in (0, 2, 1):
            parts = [
                lax.dot_general(
                    grad,
                    v.bank[e, 3 * da + db],
                    (((1,), (1,)), ((), ())),
                    preferred_element_type=f32,
                )
                for db in range(3)
            ]
            total = parts[1] + sooner(parts[0]) + later(parts[2])
            total = total.astype(bf16).reshape(cap, columns, channels)
            if da == 1:
                v.bk[s] = total
            else:
                v.eo[s, da // 2] = total
        pl.when(has_above)(lambda: edge_up(go, s))
        pl.when(has_below)(lambda: edge_down(go, s))

    def rims(s):
        pl.when(has_above)(lambda: received(v.above.at[s], v.above_recv.at[s]))
        pl.when(has_below)(lambda: received(v.below.at[s], v.below_recv.at[s]))

    def spread_out(value, spots, load, f):
        found = jnp.zeros((columns, channels), bf16)
        for c in range(cap):
            found = jnp.where(spots[c] == f, load(c), found)
        return value + found.astype(f32)

    def back_rows(s):
        mine = places(s, x)
        upper = [jnp.where(has_above, p, -1) for p in tile_places(t_above, s)]
        lower = [jnp.where(has_below, p, -1) for p in tile_places(t_below, s)]

        def row(f):
            value = jnp.zeros((columns, channels), f32)
            value = spread_out(value, mine, lambda c: v.bk[s, c], f)
            value = spread_out(value, upper, lambda c: v.above[s, c], f)
            return spread_out(value, lower, lambda c: v.below[s, c], f)

        return row

    def to_side(s, zs, xj):
        rims(s)
        row = back_rows(s)
        for f in range(frames):
            v.sbo[xj - 1, zs, f] = row(f).astype(bf16)
        side_back(go, s, zs, xj)

    def far_act(s, zs, xj):
        for j in range(1, across):
            received(v.sai.at[j - 1, zs], v.sa_recv.at[j - 1, zs])
        spots = [places(s, x)] + [
            places(s, lax.rem(x + across - j, across)) for j in range(1, across)
        ]
        for f in range(frames):
            value = spread_out(
                jnp.zeros((columns, channels), f32), spots[0], lambda c: v.act[s, c], f
            )
            for j in range(1, across):
                value = spread_out(value, spots[j], lambda c: v.sai[j - 1, zs, c], f)
            v.total[1, f] = value

        @pl.when(zs == z)
        def _():
            for f in range(frames):
                v.base[1, f] = v.total[1, f] + v.f[me, t, f].astype(f32)

        @pl.when(zs != z)
        def _():
            v.fo[zs, 1] = v.total[1].astype(bf16)
            far_terms(go, zs, 1)

    def far_back(s, zs, xj):
        rims(s)
        for j in range(1, across):
            received(v.sbi.at[j - 1, zs], v.sb_recv.at[j - 1, zs])
        row = back_rows(s)
        for f in range(frames):
            value = row(f)
            for j in range(1, across):
                value = value + v.sbi[j - 1, zs, f].astype(f32)
            v.total[0, f] = value

        @pl.when(zs == z)
        def _():
            for f in range(frames):
                v.base[0, f] = v.total[0, f] + v.c[me, f].astype(f32)

        @pl.when(zs != z)
        def _():
            v.fo[zs, 0] = v.total[0].astype(bf16)
            far_terms(go, zs, 0)

    lane = lax.broadcasted_iota(jnp.int32, (1, rows), 1) % columns

    def weigh(s, zs, xj):
        gather_passed(s)
        received(v.gi.at[s, pl.ds(0, tiles - 1)], v.g_recv.at[s])
        for tt in range(tiles):
            e = v.ts[tt, s, x, 0, 0]
            spots = tile_places(tt, s)
            span = slice(tt * rows, (tt + 1) * rows)
            for da in range(3):
                source = tt + da - 1
                if 0 <= source < tiles:
                    parts = picked(spots, lambda f: v.f[s, source, f])
                    v.xw[da, span] = jnp.concatenate(parts, axis=0)
                else:
                    v.xw[da, span] = jnp.zeros((rows, channels), bf16)
            g = v.gi[s, tt].astype(f32)
            moved = [
                jnp.where(lane == columns - 1, 0.0, pltpu.roll(g, rows - 1, 1)).astype(bf16),
                v.gi[s, tt],
                jnp.where(lane == 0, 0.0, pltpu.roll(g, 1, 1)).astype(bf16),
            ]
            for db in range(3):
                for k in range(experts):
                    first = (db * experts + k) * share
                    v.gt[first : first + share, span] = jnp.where(
                        e == k, moved[db], jnp.zeros_like(moved[db])
                    )
        for da in range(3):
            term = jnp.dot(v.gt[...], v.xw[da], preferred_element_type=f32)
            term = term.reshape(3, experts, share, channels)
            for db in range(3):
                grad_ref[:, 3 * da + db] += term[db]

    @pl.loop(0, count + count)
    def _(n):
        pl.when(n == step)(load_bank.wait)
        pl.when(n == (step + 3))(settle)
        stage(n - step, compute)
        stage(n - (step + 3), to_side, lead=False)
        stage(n - 4 * step, far_act, lead=True)
        stage(n - count, far_back, lead=True)
        stage(n - count, lambda s, zs, xj: far_rows(go, s))
        pl.when(n > 1)(lambda: stage(n, arrive))

    @pl.loop(0, count + 2)
    def _(n):
        stage(n, lambda s, zs, xj: gather_far(s))
        stage(n - 2, weigh)

    some = pl.ds(0, owners - 1)
    received(v.gated.at[some], v.gate_recv.at[0])
    sent(v.gate.at[some], v.gate_send.at[0])
    for f in range(frames):
        at = jnp.full((1, 128), -1, jnp.int32)
        for j in range(slots):
            at = jnp.where(lanes == j, owner_at(f, j), at)
        found = jnp.zeros((1, 128), f32)
        for o in range(owners):
            for c in range(cap):
                owner = jnp.where(v.os[o, 0, 1 + c] == f, o, -2)
                found = jnp.where(at == owner, v.gated[o, c : c + 1], found)
        gate_ref[f] = found[:, :slots]
    sent(v.n.at[some], v.note_send.at[0])
    sent(v.w.at[some], v.note_send.at[1])
    sent(v.tn.at[pl.ds(0, tiles - 1)], v.tn_send.at[0])

    def finish(s, zs, xj):
        @pl.when(xj == 0)
        def _():
            along(drain, s, zs, v.f.at[s, t], v.c.at[s])
            side_frames(drain, s, zs, v.f.at[s, t])
            side_packed(drain, s, zs)
            for part in range(2):
                pl.when(zs != z)(lambda part=part: far_terms(drain, zs, part))

        @pl.when(xj > 0)
        def _():
            side_act(drain, s, zs, xj)
            side_back(drain, s, zs, xj)

        near_rows(drain, s, v.f.at[s, t])
        far_rows(drain, s)
        pass_on(drain, s)
        sent(v.go.at[s, pl.ds(0, tiles - 1)], v.g_send.at[s])
        pl.when(has_above)(lambda: edge_up(drain, s))
        pl.when(has_below)(lambda: edge_down(drain, s))

    @pl.loop(0, count)
    def _(n):
        stage(n, finish)

    far_act(me, z, 0)
    far_back(me, z, 0)
    for k in range(1, deep):
        zs = lax.rem(z + k, deep)
        for part in range(2):
            received(v.fi.at[zs, part], v.fi_recv.at[part, zs])
    for f in range(frames):
        first, second = v.base[0, f], v.base[1, f]
        for k in range(1, deep):
            zs = lax.rem(z + k, deep)
            first = first + v.fi[zs, 0, f].astype(f32)
            second = second + v.fi[zs, 1, f].astype(f32)
        input_ref[f] = first.astype(bf16)
        result_ref[f] = second.astype(bf16)


def layer(frames, cot, ids, counts, gates, kernels, owners, tiles):
    deep, across = grid_of(owners)
    cores = 1 if tiles % 2 else 2
    high = tiles // cores
    count, columns, channels = frames.shape
    experts, taps, _, outputs = kernels.shape
    share = outputs // tiles
    cap = CAP
    rows = cap * columns
    dma = pltpu.SemaphoreType.DMA
    vmem, hbm = pl.BlockSpec(memory_space=pltpu.VMEM), pl.BlockSpec(memory_space=pltpu.HBM)
    bf16, f32, i32 = jnp.bfloat16, jnp.float32, jnp.int32
    beside, mates, far = (max(value - 1, 1) for value in (across, cores, high))
    scratch = dict(
        f=pltpu.VMEM((owners, tiles, count, columns, channels), bf16),
        c=pltpu.VMEM((owners, count, columns, channels), bf16),
        cp=pltpu.VMEM((owners, cap, columns, channels), bf16),
        cpo=pltpu.VMEM((beside, deep, cap, columns, channels), bf16),
        n=pltpu.VMEM((owners, across, 1, 128), i32),
        w=pltpu.VMEM((owners, 1, 128), f32),
        tn=pltpu.VMEM((tiles, owners, across, 1, 128), i32),
        os=pltpu.SMEM((owners, 1, 128), i32),
        ns=pltpu.SMEM((owners, across, 1, 128), i32),
        ws=pltpu.SMEM((owners, 1, 128), f32),
        ts=pltpu.SMEM((tiles, owners, across, 1, 128), i32),
        bank=pltpu.VMEM(kernels.shape, bf16),
        act=pltpu.VMEM((owners, cap, columns, channels), bf16),
        bk=pltpu.VMEM((owners, cap, columns, channels), bf16),
        eo=pltpu.VMEM((owners, 2, cap, columns, channels), bf16),
        above=pltpu.VMEM((owners, cap, columns, channels), bf16),
        below=pltpu.VMEM((owners, cap, columns, channels), bf16),
        go=pltpu.VMEM((owners, tiles, share, rows), bf16),
        gi=pltpu.VMEM((owners, tiles, share, rows), bf16),
        gate=pltpu.VMEM((owners, 8, 128), f32),
        gated=pltpu.VMEM((owners, 8, 128), f32),
        ids=pltpu.SMEM(ids.shape, i32),
        counts=pltpu.SMEM(counts.shape, i32),
        gates=pltpu.SMEM(gates.shape, f32),
        note=pltpu.VMEM((owners, 1, 128), i32),
        weight=pltpu.VMEM((owners, 1, 128), f32),
        sbo=pltpu.VMEM((beside, deep, count, columns, channels), bf16),
        sbi=pltpu.VMEM((beside, deep, count, columns, channels), bf16),
        sai=pltpu.VMEM((beside, deep, cap, columns, channels), bf16),
        fo=pltpu.VMEM((deep, 2, count, columns, channels), bf16),
        fi=pltpu.VMEM((deep, 2, count, columns, channels), bf16),
        total=pltpu.VMEM((2, count, columns, channels), f32),
        base=pltpu.VMEM((2, count, columns, channels), f32),
        xw=pltpu.VMEM((3, tiles * rows, channels), bf16),
        gt=pltpu.VMEM((3 * experts * share, tiles * rows), bf16),
        local_sem=dma((6,)),
        spare_sem=dma((1,)),
        note_send=dma((2,)), note_recv=dma((2,)),
        tn_send=dma((1,)), tn_recv=dma((1,)),
        f_up=dma((deep,)), f_down=dma((deep,)), f_side=dma((beside, deep)), f_recv=dma((owners,)),
        c_up=dma((deep,)), c_down=dma((deep,)), c_recv=dma((deep,)),
        cp_send=dma((beside, deep)), cp_recv=dma((owners,)),
        near_send=dma((2, owners)), far_send=dma((far, owners)),
        pass_send=dma((far, cores, mates, owners)), ft_recv=dma((owners, tiles)),
        above_send=dma((owners,)), above_recv=dma((owners,)),
        below_send=dma((owners,)), below_recv=dma((owners,)),
        g_send=dma((owners,)), g_recv=dma((owners,)),
        gate_send=dma((1,)), gate_recv=dma((1,)),
        sb_send=dma((beside, deep)), sb_recv=dma((beside, deep)),
        sa_send=dma((beside, deep)), sa_recv=dma((beside, deep)),
        fo_send=dma((2, deep)), fi_recv=dma((2, deep)),
    )
    held = 2 * frames.size * 4 * 2 + experts * taps * share * channels * 4 + owners * 8 * 128 * 4
    for ref in scratch.values():
        if ref.memory_space == pltpu.VMEM:
            held += math.prod(ref.shape) * jnp.dtype(ref.dtype).itemsize
    return pl.pallas_call(
        functools.partial(layer_kernel, deep, across, high, cores, tuple(scratch)),
        out_shape=[
            jax.ShapeDtypeStruct(frames.shape, bf16),
            jax.ShapeDtypeStruct(frames.shape, bf16),
            jax.ShapeDtypeStruct(gates.shape, f32),
            jax.ShapeDtypeStruct((experts, taps, share, channels), f32),
        ],
        in_specs=[hbm] * 6,
        out_specs=[vmem] * 4,
        scratch_shapes=list(scratch.values()),
        compiler_params=pltpu.CompilerParams(
            collective_id=0, has_side_effects=True, vmem_limit_bytes=held + (8 << 20)
        ),
        name="layer",
    )(
        *(
            pltpu.with_memory_space_constraint(value, pltpu.HBM)
            for value in (frames, cot, ids, counts, gates, kernels)
        )
    )


def settle_kernel(count, *refs):
    sems = refs[2 * count]
    copies = [
        pltpu.make_async_copy(refs[i], refs[count + i], sems.at[i]) for i in range(count)
    ]
    for copy in copies:
        copy.start()
    for copy in copies:
        copy.wait()


def settled(*arrays):
    count = len(arrays)
    anywhere = pl.BlockSpec(memory_space=pl.ANY)
    return pl.pallas_call(
        functools.partial(settle_kernel, count),
        out_shape=[jax.ShapeDtypeStruct(a.shape, a.dtype) for a in arrays],
        in_specs=[anywhere] * count,
        out_specs=[pl.BlockSpec(memory_space=pltpu.HBM)] * count,
        scratch_shapes=[pltpu.SemaphoreType.DMA((count,))],
        compiler_params=pltpu.CompilerParams(vmem_limit_bytes=1 << 20),
        name="settled",
    )(*arrays)


def shards(frames, kernels, experts, counts, gate_weights, cotangent):
    owners = lax.axis_size("dp")
    tiles = lax.axis_size("tile")
    result, input_grad, gate_grad, kernel_part = settled(
        *layer(
            frames[:, 0], cotangent[:, 0], experts, counts.T, gate_weights, kernels, owners, tiles
        )
    )
    kernel_part = jnp.swapaxes(kernel_part, 2, 3)
    return (result[:, None], input_grad[:, None], gate_grad, kernel_part)


def solution(mesh):
    return jax.shard_map(
        shards,
        mesh=mesh,
        in_specs=(
            P("dp", "tile", None, None),
            P("dp", None, None, None),
            P("dp", "tile", None),
            P("dp", "tile"),
            P("dp", "tile", None),
            P("dp", "tile", None, None),
        ),
        out_specs=(
            P("dp", "tile", None, None),
            P("dp", "tile", None, None),
            P("dp", "tile", None),
            P("dp", None, None, "tile"),
        ),
        check_vma=False,
    )
```
